256 devices in a mesh: leaf: 128 (over y, x, z), sub: 2 (over core).
Axes of the slice: x: 4, y: 4, z: 8, core: 2. Of those that a mesh axis runs over, the one named last changes fastest.
Arguments:
- density: bfloat16 [1024, 256, 32], P('leaf', None, 'sub'), may hold values from -6 to 6
- near_blocks: bfloat16 [1024, 6, 256, 256], P('leaf', 'sub'), may hold values from -0.15625 to 0.15625
- near_index: int32 [1024, 6], P('leaf', 'sub'), may hold values from 0 to 1023, as said below
- col_basis: bfloat16 [1024, 256, 64], P('leaf'), may hold values from -0.375 to 0.375
- row_basis: bfloat16 [1024, 256, 64], P('leaf'), may hold values from -0.75 to 0.75
- leaf_coupling: bfloat16 [1024, 6, 64, 64], P('leaf', 'sub'), may hold values from -0.3125 to 0.3125
- leaf_list: int32 [1024, 6], P('leaf', 'sub'), may hold values from 0 to 1023, as said below
- leaf_up: bfloat16 [1024, 64, 64], P('leaf'), may hold values from -0.25 to 0.25
- leaf_down: bfloat16 [1024, 64, 64], P('leaf'), may hold values from -0.75 to 0.75
- node_coupling: bfloat16 [128, 4, 64, 64], P('leaf'), may hold values from -0.375 to 0.375
- node_list: int32 [128, 4], P('leaf'), may hold values from 0 to 127, as said below
- node_up: bfloat16 [128, 64, 64], P('leaf'), may hold values from -0.5 to 0.5
- node_down: bfloat16 [128, 64, 64], P('leaf'), may hold values from -0.75 to 0.75
- upper_coupling: bfloat16 [126, 4, 64, 64], replicated, may hold values from -0.375 to 0.375
- upper_list: int32 [126, 4], replicated, may hold values from 2 to 127, as said below
- upper_up: bfloat16 [124, 64, 64], replicated, may hold values from -0.5 to 0.5
- upper_down: bfloat16 [124, 64, 64], replicated, may hold values from -0.75 to 0.75
Outputs:
- potential: bfloat16 [1024, 256, 32], P('leaf', None, 'sub')
The draws below stay inside these ranges and needn't reach their ends.
Inputs may be any that keep to these rules, and one draw needn't show every extreme that they name: `near_index`: row t holds 6 different leaves, the first being t itself; all lie among the leaves of t's own block of 8 and of the blocks just before and after it; none stands in row t of leaf_list. `leaf_list`: row t holds 6 different leaves other than t, all among the leaves of t's own block of 8 and of the blocks just before and after it. `node_list`: row d holds 4 different clusters other than d; the first is (d + 64) mod 128. `upper_list`: row n - 2 names nodes of node n's level other than n, possibly repeated; the first is the node half that level's size away.
All inputs are finite; a program needn't handle non-finite values.
Results may differ from the reference program's by a relative error of at most 0.029.
Values may be sent and summed in bfloat16 or wider, within the bound.
A program may use at most 128 MiB of HBM per device.

```python
import jax
import jax.numpy as jnp
from jax import lax

LEAF = 256
RANK = 64
RHS = 32
LEAF_DEV = 8
NEAR = 6
FAR = 6
FARC = 4
NODES = 128
LEAVES = 1024
UPPER = 126
INNER = 124


def leaf_pattern(key):
    window = 3 * LEAF_DEV
    leaves = jnp.arange(LEAVES, dtype=jnp.int32)
    lowest = leaves // LEAF_DEV * LEAF_DEV - LEAF_DEV
    offsets = jnp.arange(window, dtype=jnp.int32)
    trial_cluster = lowest[:, None] + offsets[None, :]
    usable = (trial_cluster >= 0) & (trial_cluster < LEAVES) & (trial_cluster != leaves[:, None])
    scores = jax.random.randint(jax.random.fold_in(key, 11), (LEAVES, window), 0, 1 << 20, dtype=jnp.int32) * window + offsets[None, :]
    scores = jnp.where(usable, scores, (1 << 20) * window + offsets[None, :])
    ranking = jnp.argsort(scores, axis=1, stable=True)
    selected_nodes = jnp.take_along_axis(trial_cluster, ranking, axis=1)
    nearby = jnp.concatenate([leaves[:, None], selected_nodes[:, :NEAR - 1]], axis=1)
    distant = selected_nodes[:, NEAR - 1:NEAR - 1 + FAR]
    return (nearby.astype(jnp.int32), distant.astype(jnp.int32))


def draw_near_index(key, part):
    return leaf_pattern(key)[0]


def draw_leaf_list(key, part):
    return leaf_pattern(key)[1]


def draw_node_list(key, part):
    clusters = jnp.arange(NODES, dtype=jnp.int32)
    offsets = jnp.arange(1, NODES, dtype=jnp.int32)
    scores = jax.random.randint(jax.random.fold_in(key, 23), (NODES, NODES - 1), 0, 1 << 20, dtype=jnp.int32) * NODES + offsets[None, :]
    scores = jnp.where(offsets[None, :] == NODES // 2, (1 << 20) * NODES + offsets[None, :], scores)
    ranking = jnp.argsort(scores, axis=1, stable=True)
    chosen = offsets[ranking[:, :FARC - 1]]
    others = (clusters[:, None] + chosen) % NODES
    leading = (clusters + NODES // 2) % NODES
    return jnp.concatenate([leading[:, None], others], axis=1).astype(jnp.int32)


def draw_upper_list(key, part):
    nodes_here = jnp.arange(2, NODES, dtype=jnp.int32)
    level_start = jnp.ones_like(nodes_here)
    for bit_pos in range(1, 24):
        level_start = jnp.where(nodes_here >= 2 ** bit_pos, 2 ** bit_pos, level_start)
    position = nodes_here - level_start
    leading = level_start + (position + level_start // 2) % level_start
    raw_steps = jax.random.randint(jax.random.fold_in(key, 37), (UPPER, FARC - 1), 0, 1 << 20, dtype=jnp.int32)
    advance = raw_steps % jnp.maximum(level_start - 1, 1)[:, None] + 1
    others = level_start[:, None] + (position[:, None] + advance) % level_start[:, None]
    return jnp.concatenate([leading[:, None], others], axis=1).astype(jnp.int32)


def steps_of(stream_key, dims, shards, low, high):
    loudness, own = 1.0, jax.random.fold_in(stream_key, 6)
    for dim, shards_of in shards:
        draws = jnp.exp(jax.random.uniform(jax.random.fold_in(own, dim), (shards_of,), jnp.float32, low / len(shards), high / len(shards)))
        loudness = loudness * jnp.repeat(draws, dims[dim] // shards_of).reshape([-1 if axis == dim else 1 for axis in range(len(dims))])
    return loudness


def centred(stream_key, extent, deviation, most, cuts=(), kind=jnp.bfloat16):
    entries = deviation * jax.random.normal(stream_key, extent, jnp.float32)
    if cuts:
        entries = entries * steps_of(stream_key, extent, cuts, -0.22, 0.18)
    return jnp.clip(entries, -most, most).astype(kind)


def setup_inputs(seed: int = 0) -> dict:
    key_list = jax.random.split(jax.random.key(seed), 18)
    density = centred(key_list[0], (LEAVES, LEAF, RHS), 1.0, 6.0, ((0, 128), (2, 2)))
    near_blocks = centred(key_list[1], (LEAVES, NEAR, LEAF, LEAF), (LEAF * NEAR) ** -0.5, 0.15625, ((0, 128), (1, 2)))
    near_index = draw_near_index(jax.random.fold_in(key_list[17], 71), 0)
    col_basis = centred(key_list[3], (LEAVES, LEAF, RANK), LEAF ** -0.5, 0.375, ((0, 128),))
    row_basis = centred(key_list[4], (LEAVES, LEAF, RANK), RANK ** -0.5, 0.75, ((0, 128),))
    leaf_coupling = centred(key_list[5], (LEAVES, FAR, RANK, RANK), (RANK * FAR) ** -0.5, 0.3125, ((0, 128), (1, 2)))
    leaf_list = draw_leaf_list(jax.random.fold_in(key_list[17], 71), 0)
    leaf_up = centred(key_list[7], (LEAVES, RANK, RANK), (RANK * LEAF_DEV) ** -0.5, 0.25, ((0, 128),))
    leaf_down = centred(key_list[8], (LEAVES, RANK, RANK), RANK ** -0.5, 0.75, ((0, 128),))
    node_coupling = centred(key_list[9], (NODES, FARC, RANK, RANK), (RANK * FARC) ** -0.5, 0.375, ((0, 128),))
    node_list = draw_node_list(jax.random.fold_in(key_list[17], 71), 0)
    node_up = centred(key_list[11], (NODES, RANK, RANK), (2 * RANK) ** -0.5, 0.5, ((0, 128),))
    node_down = centred(key_list[12], (NODES, RANK, RANK), RANK ** -0.5, 0.75, ((0, 128),))
    upper_coupling = centred(key_list[13], (UPPER, FARC, RANK, RANK), (RANK * FARC) ** -0.5, 0.375)
    upper_list = draw_upper_list(jax.random.fold_in(key_list[17], 71), 0)
    upper_up = centred(key_list[15], (INNER, RANK, RANK), (2 * RANK) ** -0.5, 0.5)
    upper_down = centred(key_list[16], (INNER, RANK, RANK), RANK ** -0.5, 0.75)
    return dict(density=density, near_blocks=near_blocks, near_index=near_index, col_basis=col_basis, row_basis=row_basis, leaf_coupling=leaf_coupling, leaf_list=leaf_list, leaf_up=leaf_up, leaf_down=leaf_down, node_coupling=node_coupling, node_list=node_list, node_up=node_up, node_down=node_down, upper_coupling=upper_coupling, upper_list=upper_list, upper_up=upper_up, upper_down=upper_down)


def upper_tree(raised_coefficients, upper_coupling, upper_list, upper_up, upper_down, node_count):
    levels = node_count.bit_length() - 1
    rank_size = raised_coefficients.shape[1]
    columns = raised_coefficients.shape[2]
    coeffs = {}
    summed = raised_coefficients.astype(jnp.float32).reshape(node_count // 2, 2, rank_size, columns).sum(axis=1)
    coeffs[levels - 1] = summed.astype(jnp.bfloat16)
    for height in range(levels - 2, 0, -1):
        lower_size = 2 ** (height + 1)
        matrices = upper_up[lower_size - 4:2 * lower_size - 4].astype(jnp.float32)
        shifted = jnp.einsum("nrs,nrc->nsc", matrices, coeffs[height + 1].astype(jnp.float32))
        coeffs[height] = shifted.reshape(lower_size // 2, 2, rank_size, columns).sum(axis=1).astype(jnp.bfloat16)
    answer = None
    for height in range(1, levels):
        breadth = 2 ** height
        listed = upper_list[breadth - 2:2 * breadth - 2] - breadth
        sources = coeffs[height][listed]
        coupled = jnp.einsum("nfrs,nfsc->nrc", upper_coupling[breadth - 2:2 * breadth - 2].astype(jnp.float32), sources.astype(jnp.float32))
        if height > 1:
            parents = jnp.repeat(answer, 2, axis=0)
            coupled = coupled + jnp.einsum("nrs,nsc->nrc", upper_down[breadth - 4:2 * breadth - 4].astype(jnp.float32), parents.astype(jnp.float32))
        answer = coupled.astype(jnp.bfloat16)
    return answer


def reference(density, near_blocks, near_index, col_basis, row_basis, leaf_coupling, leaf_list, leaf_up, leaf_down, node_coupling, node_list, node_up, node_down, upper_coupling, upper_list, upper_up, upper_down):
    leaf_coeff = jnp.einsum("tlr,tlc->trc", col_basis.astype(jnp.float32), density.astype(jnp.float32)).astype(jnp.bfloat16)
    far_sources = leaf_coeff[leaf_list]
    far_field = jnp.einsum("tjrs,tjsc->trc", leaf_coupling.astype(jnp.float32), far_sources.astype(jnp.float32))
    grouped_up = leaf_up.reshape(NODES, LEAF_DEV, RANK, RANK).astype(jnp.float32)
    grouped_coeff = leaf_coeff.reshape(NODES, LEAF_DEV, RANK, RHS).astype(jnp.float32)
    node_coeff = jnp.einsum("ntrs,ntrc->nsc", grouped_up, grouped_coeff).astype(jnp.bfloat16)
    raised_coefficients = jnp.einsum("nrs,nrc->nsc", node_up.astype(jnp.float32), node_coeff.astype(jnp.float32)).astype(jnp.bfloat16)
    answer = upper_tree(raised_coefficients, upper_coupling, upper_list, upper_up, upper_down, NODES)
    node_term = jnp.einsum("nfrs,nfsc->nrc", node_coupling.astype(jnp.float32), node_coeff[node_list].astype(jnp.float32))
    parents = jnp.repeat(answer, 2, axis=0)
    node_term = node_term + jnp.einsum("nrs,nsc->nrc", node_down.astype(jnp.float32), parents.astype(jnp.float32))
    node_field = node_term.astype(jnp.bfloat16)
    grouped_down = leaf_down.reshape(NODES, LEAF_DEV, RANK, RANK).astype(jnp.float32)
    descended = jnp.einsum("ntrs,nsc->ntrc", grouped_down, node_field.astype(jnp.float32)).reshape(LEAVES, RANK, RHS)
    leaf_field = (far_field + descended).astype(jnp.bfloat16)

    def device_near(block_number):
        row_start = block_number * LEAF_DEV
        block_entries = lax.dynamic_slice_in_dim(near_blocks, row_start, LEAF_DEV, 0)
        indices = lax.dynamic_slice_in_dim(near_index, row_start, LEAF_DEV, 0)
        selected_nodes = density[indices]
        return jnp.einsum("vpqx,vpxn->vqn", block_entries.astype(jnp.float32), selected_nodes.astype(jnp.float32))

    proximate_field = lax.map(device_near, jnp.arange(NODES, dtype=jnp.int32)).reshape(LEAVES, LEAF, RHS)
    farther = jnp.einsum("tlr,trc->tlc", row_basis.astype(jnp.float32), leaf_field.astype(jnp.float32))
    return (proximate_field + farther).astype(jnp.bfloat16)
```

```python
import jax
import jax.numpy as jnp
from jax import lax
from jax.experimental import pallas as pl
from jax.experimental.pallas import tpu as pltpu
from jax.sharding import PartitionSpec as P

MESH = pl.DeviceIdType.MESH
F32 = jnp.float32
BF16 = jnp.bfloat16

LEAVES = 8
COLS = 16
RANK = 64
RING = 8
PLANE = 16
DEVS = RING * PLANE
TILES = 9


def dot(a, b):
    return jnp.dot(a, b, preferred_element_type=F32)


def dot_nt(a, b):
    return lax.dot_general(a, b, (((1,), (1,)), ((), ())), preferred_element_type=F32)


def within(i, first, last):
    return jnp.minimum(jnp.maximum(i, first), last)


def kernel(
    dens_hbm,
    near_hbm,
    near_idx,
    colb_hbm,
    rowb_hbm,
    lcoup_hbm,
    leaf_idx,
    lup_hbm,
    ldown_hbm,
    ncoup_hbm,
    node_idx,
    nup_hbm,
    ndown_hbm,
    upc_hbm,
    upper_idx,
    upu_hbm,
    upd_hbm,
    out_ref,
    dens_win,
    near_v,
    colb_v,
    rowb_v,
    lcoup_v,
    lup_v,
    ldown_v,
    ncoup_v,
    nup_v,
    ndown_v,
    upc_v,
    upu_v,
    upd_v,
    lc_win,
    zbuf,
    tab,
    sel_up,
    sel_c,
    sel_d,
    near_own,
    near_out,
    near_in,
    far_own,
    far_out,
    far_in,
    load_sem,
    z_send,
    z_recv,
    p_send,
    p_recv,
    d_send,
    d_recv,
    l_send,
    l_recv,
    x_send,
    x_recv,
):
    leaf = lax.axis_index("leaf")
    sub = lax.axis_index("sub")
    other = 1 - sub
    group = leaf // RING
    z = leaf % RING
    mid = pl.ds(LEAVES, LEAVES)

    loads = [
        (dens_hbm, dens_win.at[mid, pl.ds(0, COLS), :]),
        (colb_hbm, colb_v),
        (lup_hbm, lup_v),
        (nup_hbm, nup_v),
        (upu_hbm, upu_v),
        (upc_hbm, upc_v),
        (near_hbm, near_v),
        (lcoup_hbm, lcoup_v),
        (upd_hbm, upd_v),
        (ndown_hbm, ndown_v),
        (ncoup_hbm, ncoup_v),
        (ldown_hbm, ldown_v),
        (rowb_hbm, rowb_v),
    ]
    load = [
        pltpu.make_async_copy(src, dst, load_sem.at[i]) for i, (src, dst) in enumerate(loads)
    ]
    for copy in load:
        copy.start()

    def ring_peer(k):
        return {"leaf": group * RING + (z + k) % RING, "sub": sub}

    def plane_peer(k):
        return {"leaf": ((group + k) % PLANE) * RING + z, "sub": sub}

    after, before = (leaf + 1) % DEVS, (leaf + DEVS - 1) % DEVS
    neighbours = [
        ({"leaf": leaf, "sub": other}, LEAVES, COLS),
        ({"leaf": after, "sub": sub}, 0, 0),
        ({"leaf": after, "sub": other}, 0, COLS),
        ({"leaf": before, "sub": sub}, 2 * LEAVES, 0),
        ({"leaf": before, "sub": other}, 2 * LEAVES, COLS),
    ]

    barrier = pltpu.get_barrier_semaphore()
    greeted = (
        [ring_peer(k) for k in range(1, RING)]
        + [plane_peer(k) for k in range(1, PLANE)]
        + [device for device, _, _ in neighbours]
    )
    for device in greeted:
        pl.semaphore_signal(barrier, inc=1, device_id=device, device_id_type=MESH)

    load[0].wait()
    load[1].wait()
    pairs = []
    for i in range(LEAVES // 2):
        halves = [
            dot_nt(dens_win[LEAVES + t, 0:COLS, :], colb_v[t]) for t in (2 * i, 2 * i + 1)
        ]
        pair = jnp.concatenate(halves, axis=1).astype(BF16)
        lc_win[LEAVES // 2 + i, 0:COLS, :] = pair
        pairs.append(pair)
    load[2].wait()
    load[3].wait()
    raw = dot(jnp.concatenate(pairs, axis=1), lup_v[...].reshape(LEAVES * RANK, RANK))
    raised = dot(raw.astype(BF16), nup_v[0])
    zbuf[z] = jnp.concatenate([raw, raised], axis=1).astype(BF16)

    pl.semaphore_wait(barrier, len(greeted))

    def ring_copy(k, slot):
        return pltpu.make_async_remote_copy(
            src_ref=zbuf.at[slot],
            dst_ref=zbuf.at[slot],
            send_sem=z_send.at[k],
            recv_sem=z_recv.at[k],
            device_id=ring_peer(k),
            device_id_type=MESH,
        )

    for k in range(1, RING):
        ring_copy(k, z).start()

    def dens_copy(i):
        device, first, row = neighbours[i]
        return pltpu.make_async_remote_copy(
            src_ref=dens_win.at[mid, pl.ds(0, COLS), :],
            dst_ref=dens_win.at[pl.ds(first, LEAVES), pl.ds(row, COLS), :],
            send_sem=d_send.at[i],
            recv_sem=d_recv.at[i],
            device_id=device,
            device_id_type=MESH,
        )

    def lc_copy(i):
        device, first, row = neighbours[i]
        return pltpu.make_async_remote_copy(
            src_ref=lc_win.at[pl.ds(LEAVES // 2, LEAVES // 2), pl.ds(0, COLS), :],
            dst_ref=lc_win.at[pl.ds(first // 2, LEAVES // 2), pl.ds(row, COLS), :],
            send_sem=l_send.at[i],
            recv_sem=l_recv.at[i],
            device_id=device,
            device_id_type=MESH,
        )

    for i in range(5):
        lc_copy(i).start()
    for i in range(5):
        dens_copy(i).start()

    def one_hot(target, count):
        column = lax.broadcasted_iota(jnp.int32, (target.shape[0], count), 1)
        return (column == target).astype(F32).astype(BF16)

    row16 = lax.broadcasted_iota(jnp.int32, (16, 1), 0)
    target = jnp.where(
        row16 < 4,
        60 + 4 * group + row16,
        jnp.where(
            row16 < 6,
            24 + 2 * group + row16,
            jnp.where(row16 == 6, 12 + group, jnp.where(row16 == 7, 4 + group // 2, group // 4)),
        ),
    )
    pick_up = one_hot(target, upu_v.shape[2])
    half = RANK // 2

    def extract(pick, source, dest, rows):
        def step(r, carry):
            slab = jnp.concatenate([source[r], source[r + half]], axis=0)
            dest[pl.ds(pl.multiple_of(r * rows, rows), rows), :] = dot_nt(pick, slab)
            return carry

        lax.fori_loop(0, half, step, 0, unroll=8)

    load[4].wait()
    extract(pick_up, upu_v, sel_up, 16)

    def matrix_up(k):
        m = sel_up[pl.ds(k, half, stride=16), :]
        return jnp.concatenate([m[:, :RANK], m[:, RANK:]], axis=0)

    blank = jnp.zeros((RANK, RANK), F32)

    def placed(m, low_in, low_out):
        wide = jnp.concatenate([m, blank] if low_out else [blank, m], axis=1)
        none = jnp.zeros((RANK, 2 * RANK), F32)
        return jnp.concatenate([wide, none] if low_in else [none, wide], axis=0).astype(BF16)

    up = [placed(matrix_up(k), False, False) for k in range(7)]
    up.append(placed(matrix_up(7), False, True))
    up.append(placed(matrix_up(8), True, False))

    for k in range(1, RING):
        ring_copy(k, (z + RING - k) % RING).wait_recv()
    held = [zbuf[i].astype(F32) for i in range(RING)]
    c64 = [held[2 * i] + held[2 * i + 1] for i in range(4)]
    b64 = [c.astype(BF16) for c in c64]
    c32 = [
        dot(
            jnp.concatenate([b64[2 * a], b64[2 * a + 1]], axis=1),
            jnp.concatenate([up[2 * a], up[2 * a + 1]], axis=0),
        )
        for a in range(2)
    ]
    c16 = dot(
        jnp.concatenate([c.astype(BF16) for c in c32], axis=1),
        jnp.concatenate([up[4], up[5]], axis=0),
    )
    c8 = dot(c16.astype(BF16), up[6])
    c4 = dot(c8.astype(BF16), up[7])
    c2 = dot(c4.astype(BF16), up[8])
    low = lax.broadcasted_iota(jnp.int32, (COLS, 2 * RANK), 1) < RANK
    for i, c in enumerate(c64 + c32 + [c16, c8]):
        tab[group, i] = jnp.where(low, held[i], c).astype(BF16)
    tab[group, 8] = (c4 + c2).astype(BF16)

    def plane_copy(k, slot):
        return pltpu.make_async_remote_copy(
            src_ref=tab.at[slot],
            dst_ref=tab.at[slot],
            send_sem=p_send.at[k],
            recv_sem=p_recv.at[k],
            device_id=plane_peer(k),
            device_id_type=MESH,
        )

    for k in range(1, PLANE):
        plane_copy(k, group).start()

    for i in range(5):
        lc_copy(i).wait_recv()
    for i in range(5):
        dens_copy(i).wait_recv()
    load[6].wait()
    load[7].wait()
    base = leaf * LEAVES - LEAVES
    for i in range(LEAVES // 2):
        far = []
        for t in (2 * i, 2 * i + 1):
            near_sum = far_sum = None
            for j in range(3):
                column = within(near_idx[j, t] - base, 0, 3 * LEAVES - 1)
                near_term = dot_nt(dens_win[column], near_v[t, j])
                near_sum = near_term if near_sum is None else near_sum + near_term
                source = within(leaf_idx[j, t] - base, 0, 3 * LEAVES - 1)
                tile = lc_win[source // 2].astype(F32)
                turned = jnp.concatenate([tile[:, RANK:], tile[:, :RANK]], axis=1)
                chosen = jnp.where(source % 2 == 1, turned, tile)[:, :RANK].astype(BF16)
                far_term = dot_nt(chosen, lcoup_v[t, j])
                far_sum = far_term if far_sum is None else far_sum + far_term
            near_own[t] = near_sum[:COLS]
            near_out[t] = near_sum[COLS:].astype(BF16)
            far.append(far_sum)
        pair = jnp.concatenate(far, axis=1)
        far_own[i] = pair[:COLS]
        far_out[i] = pair[COLS:].astype(BF16)

    partner = {"leaf": leaf, "sub": other}
    swaps = [
        pltpu.make_async_remote_copy(
            src_ref=src,
            dst_ref=dst,
            send_sem=x_send.at[i],
            recv_sem=x_recv.at[i],
            device_id=partner,
            device_id_type=MESH,
        )
        for i, (src, dst) in enumerate(((near_out, near_in), (far_out, far_in)))
    ]
    for copy in swaps:
        copy.start()

    row8 = lax.broadcasted_iota(jnp.int32, (8, 1), 0)
    top = DEVS + leaf
    node_of = jnp.zeros((8, 1), jnp.int32)
    for k in range(6):
        node_of = jnp.where(row8 == k, top // (2 << k), node_of)
    load[5].wait()
    load[8].wait()
    pick_c = one_hot(node_of - 2, upc_v.shape[3])
    pick_d = one_hot(node_of - 4, upd_v.shape[2])
    for j in range(4):
        extract(pick_c, upc_v.at[j], sel_c.at[j], 8)
    extract(pick_d, upd_v, sel_d, 8)

    low64 = lax.broadcasted_iota(jnp.int32, (RANK, 2 * RANK), 1) < RANK

    def coupling(k, low_in):
        parts = []
        for j in range(4):
            m = sel_c[j, pl.ds(k, half, stride=8), :]
            turned = jnp.concatenate([m[:, RANK:], m[:, :RANK]], axis=1)
            both = jnp.concatenate([m, turned] if low_in else [turned, m], axis=0)
            parts.append(jnp.where(low64 == low_in, both, 0.0).astype(BF16))
        return jnp.concatenate(parts, axis=1)

    couplings = [coupling(k, k == 4) for k in range(6)]
    load[9].wait()
    load[10].wait()
    blank_b = jnp.zeros((RANK, RANK), BF16)
    near_coupling = jnp.concatenate(
        [m for j in range(4) for m in (ncoup_v[0, j], blank_b)], axis=1
    )
    chain = [ndown_v[0]]
    for k in range(5):
        m = sel_d[pl.ds(k, half, stride=8), :]
        down = jnp.concatenate([m[:, :RANK], m[:, RANK:]], axis=0).astype(BF16)
        chain.append(dot(chain[-1], down).astype(BF16))
    load[11].wait()
    load[12].wait()

    for k in range(1, PLANE):
        plane_copy(k, (group + PLANE - k) % PLANE).wait_recv()

    def source_tile(k, j):
        n = within(upper_idx[j, top // (2 << k) - 2], 64 >> k, (128 >> k) - 1)
        if k == 0:
            return tab[(n - 64) // 4, n % 4]
        if k == 1:
            return tab[(n - 32) // 2, 4 + n % 2]
        if k == 2:
            return tab[n - 16, 6]
        count = 1 << (k - 2)
        first = (n - (64 >> k)) * count
        total = None
        for i in range(count):
            part = tab[first + i, 7 if k == 3 else 8].astype(F32)
            total = part if total is None else total + part
        return total.astype(BF16)

    def node_tile(j):
        n = within(node_idx[0, j], 0, DEVS - 1)
        return tab[n // RING, n % RING]

    field = dot_nt(jnp.concatenate([node_tile(j) for j in range(4)], axis=1), near_coupling)
    for k in range(6):
        part = dot_nt(
            jnp.concatenate([source_tile(k, j) for j in range(4)], axis=1), couplings[k]
        )
        field = field + dot_nt(part.astype(BF16), chain[k])
    descended = dot_nt(field.astype(BF16), ldown_v[...].reshape(LEAVES * RANK, RANK))

    for copy in swaps:
        copy.wait_recv()
    for i in range(LEAVES // 2):
        pair = descended[:, 2 * RANK * i : 2 * RANK * (i + 1)]
        pair = pair + far_own[i] + far_in[i].astype(F32)
        stacked = jnp.concatenate(
            [jnp.where(low, pair, 0.0), jnp.where(low, 0.0, pair)], axis=0
        ).astype(BF16)
        farther = dot(stacked, rowb_v[2 * i : 2 * i + 2].reshape(2 * RANK, rowb_v.shape[2]))
        for h in range(2):
            t = 2 * i + h
            total = farther[h * COLS : (h + 1) * COLS] + near_own[t] + near_in[t].astype(F32)
            out_ref[t] = total.astype(BF16)

    for k in range(1, RING):
        ring_copy(k, z).wait_send()
    for k in range(1, PLANE):
        plane_copy(k, group).wait_send()
    for i in range(5):
        dens_copy(i).wait_send()
        lc_copy(i).wait_send()
    for copy in swaps:
        copy.wait_send()


def body(
    density,
    near_blocks,
    near_index,
    col_basis,
    row_basis,
    leaf_coupling,
    leaf_list,
    leaf_up,
    leaf_down,
    node_coupling,
    node_list,
    node_up,
    node_down,
    upper_coupling,
    upper_list,
    upper_up,
    upper_down,
):
    args = (
        jnp.swapaxes(density, 1, 2),
        near_blocks,
        near_index.T,
        jnp.swapaxes(col_basis, 1, 2),
        jnp.swapaxes(row_basis, 1, 2),
        leaf_coupling,
        leaf_list.T,
        leaf_up,
        leaf_down,
        node_coupling,
        node_list,
        node_up,
        node_down,
        jnp.transpose(upper_coupling, (1, 2, 3, 0)),
        upper_list.T,
        jnp.transpose(upper_up, (1, 2, 0)),
        jnp.transpose(upper_down, (1, 2, 0)),
    )
    held = pl.BlockSpec(memory_space=pltpu.HBM)
    small = pl.BlockSpec(memory_space=pltpu.SMEM)
    specs = [small if a.dtype == jnp.int32 else held for a in args]
    points = density.shape[1]
    dma = pltpu.SemaphoreType.DMA

    def like(i):
        return pltpu.VMEM(args[i].shape, args[i].dtype)

    result = pl.pallas_call(
        kernel,
        out_shape=jax.ShapeDtypeStruct((LEAVES, COLS, points), BF16),
        in_specs=specs,
        out_specs=pl.BlockSpec(memory_space=pltpu.VMEM),
        scratch_shapes=[
            pltpu.VMEM((3 * LEAVES, 2 * COLS, points), BF16),
            like(1),
            like(3),
            like(4),
            like(5),
            like(7),
            like(8),
            like(9),
            like(11),
            like(12),
            like(13),
            like(15),
            like(16),
            pltpu.VMEM((3 * LEAVES // 2, 2 * COLS, 2 * RANK), BF16),
            pltpu.VMEM((RING, COLS, 2 * RANK), BF16),
            pltpu.VMEM((PLANE, TILES, COLS, 2 * RANK), BF16),
            pltpu.VMEM((16 * RANK // 2, 2 * RANK), F32),
            pltpu.VMEM((4, 8 * RANK // 2, 2 * RANK), F32),
            pltpu.VMEM((8 * RANK // 2, 2 * RANK), F32),
            pltpu.VMEM((LEAVES, COLS, points), F32),
            pltpu.VMEM((LEAVES, COLS, points), BF16),
            pltpu.VMEM((LEAVES, COLS, points), BF16),
            pltpu.VMEM((LEAVES // 2, COLS, 2 * RANK), F32),
            pltpu.VMEM((LEAVES // 2, COLS, 2 * RANK), BF16),
            pltpu.VMEM((LEAVES // 2, COLS, 2 * RANK), BF16),
            dma((13,)),
            dma((RING,)),
            dma((RING,)),
            dma((PLANE,)),
            dma((PLANE,)),
            dma((5,)),
            dma((5,)),
            dma((5,)),
            dma((5,)),
            dma((2,)),
            dma((2,)),
        ],
        compiler_params=pltpu.CompilerParams(
            collective_id=0, has_side_effects=True, vmem_limit_bytes=60 << 20
        ),
        name="product",
    )(*args)
    return jnp.swapaxes(result, 1, 2)


def solution(mesh):
    placed = (
        P("leaf", None, "sub"),
        P("leaf", "sub", None, None),
        P("leaf", "sub"),
        P("leaf", None, None),
        P("leaf", None, None),
        P("leaf", "sub", None, None),
        P("leaf", "sub"),
        P("leaf", None, None),
        P("leaf", None, None),
        P("leaf", None, None, None),
        P("leaf", None),
        P("leaf", None, None),
        P("leaf", None, None),
        P(),
        P(),
        P(),
        P(),
    )
    return jax.shard_map(
        body, mesh=mesh, in_specs=placed, out_specs=P("leaf", None, "sub"), check_vma=False
    )
```

```python
import jax
import jax.numpy as jnp
from jax import lax
from jax.experimental import pallas as pl
from jax.experimental.pallas import tpu as pltpu
from jax.sharding import PartitionSpec as P

MESH = pl.DeviceIdType.MESH
F32 = jnp.float32
BF16 = jnp.bfloat16

LEAVES = 8
COLS = 16
RANK = 64
RING = 8
PLANE = 16
DEVS = RING * PLANE
TILES = 9
RING_ORDER = (4, 3, 5, 2, 6, 1, 7)
PLANE_ORDER = (10, 6, 14, 9, 11, 2, 8, 5, 7, 13, 15, 1, 3, 4, 12)


def dot(a, b):
    return jnp.dot(a, b, preferred_element_type=F32)


def dot_nt(a, b):
    return lax.dot_general(a, b, (((1,), (1,)), ((), ())), preferred_element_type=F32)


def within(i, first, last):
    return jnp.minimum(jnp.maximum(i, first), last)


def kernel(
    dens_hbm,
    near_hbm,
    near_idx,
    colb_hbm,
    rowb_hbm,
    lcoup_hbm,
    leaf_idx,
    lup_hbm,
    ldown_hbm,
    ncoup_hbm,
    node_idx,
    nup_hbm,
    ndown_hbm,
    upc_hbm,
    upper_idx,
    upu_hbm,
    upd_hbm,
    out_ref,
    dens_win,
    near_v,
    colb_v,
    rowb_v,
    lcoup_v,
    lup_v,
    ldown_v,
    ncoup_v,
    nup_v,
    ndown_v,
    upc_v,
    upu_v,
    upd_v,
    lc_win,
    zbuf,
    tab,
    sel_up,
    sel_c,
    sel_d,
    near_own,
    near_out,
    near_in,
    far_own,
    far_out,
    far_in,
    load_sem,
    z_send,
    z_recv,
    p_send,
    p_recv,
    d_send,
    d_recv,
    l_send,
    l_recv,
    x_send,
    x_recv,
):
    leaf = lax.axis_index("leaf")
    sub = lax.axis_index("sub")
    other = 1 - sub
    group = leaf // RING
    z = leaf % RING
    mid = pl.ds(LEAVES, LEAVES)

    loads = [
        (dens_hbm, dens_win.at[mid, pl.ds(0, COLS), :]),
        (colb_hbm, colb_v),
        (lup_hbm, lup_v),
        (nup_hbm, nup_v),
        (upu_hbm, upu_v),
        (upc_hbm, upc_v),
        (near_hbm, near_v),
        (lcoup_hbm, lcoup_v),
        (upd_hbm, upd_v),
        (ndown_hbm, ndown_v),
        (ncoup_hbm, ncoup_v),
        (ldown_hbm, ldown_v),
        (rowb_hbm, rowb_v),
    ]
    load = [
        pltpu.make_async_copy(src, dst, load_sem.at[i]) for i, (src, dst) in enumerate(loads)
    ]
    for copy in load[:5]:
        copy.start()

    def ring_peer(k):
        return {"leaf": group * RING + (z + k) % RING, "sub": sub}

    def plane_peer(k):
        return {"leaf": ((group + k) % PLANE) * RING + z, "sub": sub}

    after, before = (leaf + 1) % DEVS, (leaf + DEVS - 1) % DEVS
    partner = {"leaf": leaf, "sub": other}
    moves = [
        ({"leaf": after, "sub": sub}, LEAVES, 0, 0),
        ({"leaf": before, "sub": sub}, LEAVES, 2 * LEAVES, 0),
        (partner, LEAVES, LEAVES, COLS),
        (partner, 0, 0, COLS),
        (partner, 2 * LEAVES, 2 * LEAVES, COLS),
    ]

    barrier = pltpu.get_barrier_semaphore()
    greeted = (
        [ring_peer(k) for k in RING_ORDER]
        + [plane_peer(k) for k in PLANE_ORDER]
        + [device for device, _, _, _ in moves[:3]]
    )
    for device in greeted:
        pl.semaphore_signal(barrier, inc=1, device_id=device, device_id_type=MESH)

    load[0].wait()
    load[1].wait()
    pairs = []
    for i in range(LEAVES // 2):
        halves = [
            dot_nt(dens_win[LEAVES + t, 0:COLS, :], colb_v[t]) for t in (2 * i, 2 * i + 1)
        ]
        pair = jnp.concatenate(halves, axis=1).astype(BF16)
        lc_win[LEAVES // 2 + i, 0:COLS, :] = pair
        pairs.append(pair)
    load[2].wait()
    load[3].wait()
    for copy in load[5:]:
        copy.start()
    raw = dot(jnp.concatenate(pairs, axis=1), lup_v[...].reshape(LEAVES * RANK, RANK))
    raised = dot(raw.astype(BF16), nup_v[0])
    zbuf[z] = jnp.concatenate([raw, raised], axis=1).astype(BF16)

    pl.semaphore_wait(barrier, len(greeted))

    def ring_copy(k, slot):
        return pltpu.make_async_remote_copy(
            src_ref=zbuf.at[slot],
            dst_ref=zbuf.at[slot],
            send_sem=z_send.at[k],
            recv_sem=z_recv.at[k],
            device_id=ring_peer(k),
            device_id_type=MESH,
        )

    for k in RING_ORDER:
        ring_copy(k, z).start()

    def dens_copy(i):
        device, here, there, row = moves[i]
        return pltpu.make_async_remote_copy(
            src_ref=dens_win.at[pl.ds(here, LEAVES), pl.ds(0, COLS), :],
            dst_ref=dens_win.at[pl.ds(there, LEAVES), pl.ds(row, COLS), :],
            send_sem=d_send.at[i],
            recv_sem=d_recv.at[i],
            device_id=device,
            device_id_type=MESH,
        )

    def lc_copy(i):
        device, here, there, row = moves[i]
        return pltpu.make_async_remote_copy(
            src_ref=lc_win.at[pl.ds(here // 2, LEAVES // 2), pl.ds(0, COLS), :],
            dst_ref=lc_win.at[pl.ds(there // 2, LEAVES // 2), pl.ds(row, COLS), :],
            send_sem=l_send.at[i],
            recv_sem=l_recv.at[i],
            device_id=device,
            device_id_type=MESH,
        )

    for i in range(3):
        lc_copy(i).start()
        dens_copy(i).start()

    def one_hot(target, count):
        column = lax.broadcasted_iota(jnp.int32, (target.shape[0], count), 1)
        return (column == target).astype(F32).astype(BF16)

    row16 = lax.broadcasted_iota(jnp.int32, (16, 1), 0)
    target = jnp.where(
        row16 < 4,
        60 + 4 * group + row16,
        jnp.where(
            row16 < 6,
            24 + 2 * group + row16,
            jnp.where(row16 == 6, 12 + group, jnp.where(row16 == 7, 4 + group // 2, group // 4)),
        ),
    )
    pick_up = one_hot(target, upu_v.shape[2])
    half = RANK // 2

    def extract(pick, source, dest, rows):
        def step(r, carry):
            slab = jnp.concatenate([source[r], source[r + half]], axis=0)
            dest[pl.ds(pl.multiple_of(r * rows, rows), rows), :] = dot_nt(pick, slab)
            return carry

        lax.fori_loop(0, half, step, 0, unroll=8)

    load[4].wait()
    extract(pick_up, upu_v, sel_up, 16)

    def matrix_up(k):
        m = sel_up[pl.ds(k, half, stride=16), :]
        return jnp.concatenate([m[:, :RANK], m[:, RANK:]], axis=0)

    blank = jnp.zeros((RANK, RANK), F32)

    def placed(m, low_in, low_out):
        wide = jnp.concatenate([m, blank] if low_out else [blank, m], axis=1)
        none = jnp.zeros((RANK, 2 * RANK), F32)
        return jnp.concatenate([wide, none] if low_in else [none, wide], axis=0).astype(BF16)

    up = [placed(matrix_up(k), False, False) for k in range(7)]
    up.append(placed(matrix_up(7), False, True))
    up.append(placed(matrix_up(8), True, False))

    for k in range(1, RING):
        ring_copy(k, (z + RING - k) % RING).wait_recv()
    held = [zbuf[i].astype(F32) for i in range(RING)]
    c64 = [held[2 * i] + held[2 * i + 1] for i in range(4)]
    b64 = [c.astype(BF16) for c in c64]
    c32 = [
        dot(
            jnp.concatenate([b64[2 * a], b64[2 * a + 1]], axis=1),
            jnp.concatenate([up[2 * a], up[2 * a + 1]], axis=0),
        )
        for a in range(2)
    ]
    c16 = dot(
        jnp.concatenate([c.astype(BF16) for c in c32], axis=1),
        jnp.concatenate([up[4], up[5]], axis=0),
    )
    c8 = dot(c16.astype(BF16), up[6])
    c4 = dot(c8.astype(BF16), up[7])
    c2 = dot(c4.astype(BF16), up[8])
    low = lax.broadcasted_iota(jnp.int32, (COLS, 2 * RANK), 1) < RANK
    for i, c in enumerate(c64 + c32 + [c16, c8]):
        tab[group, i] = jnp.where(low, held[i], c).astype(BF16)
    tab[group, 8] = (c4 + c2).astype(BF16)

    def plane_copy(k, slot):
        return pltpu.make_async_remote_copy(
            src_ref=tab.at[slot],
            dst_ref=tab.at[slot],
            send_sem=p_send.at[k],
            recv_sem=p_recv.at[k],
            device_id=plane_peer(k),
            device_id_type=MESH,
        )

    for k in PLANE_ORDER:
        plane_copy(k, group).start()
    for i in range(2):
        lc_copy(i).wait_recv()
        lc_copy(3 + i).start()
        dens_copy(i).wait_recv()
        dens_copy(3 + i).start()

    row8 = lax.broadcasted_iota(jnp.int32, (8, 1), 0)
    top = DEVS + leaf
    node_of = jnp.zeros((8, 1), jnp.int32)
    for k in range(6):
        node_of = jnp.where(row8 == k, top // (2 << k), node_of)
    load[5].wait()
    load[8].wait()
    pick_c = one_hot(node_of - 2, upc_v.shape[3])
    pick_d = one_hot(node_of - 4, upd_v.shape[2])
    for j in range(4):
        extract(pick_c, upc_v.at[j], sel_c.at[j], 8)
    extract(pick_d, upd_v, sel_d, 8)

    low64 = lax.broadcasted_iota(jnp.int32, (RANK, 2 * RANK), 1) < RANK

    def coupling(k, low_in):
        parts = []
        for j in range(4):
            m = sel_c[j, pl.ds(k, half, stride=8), :]
            turned = jnp.concatenate([m[:, RANK:], m[:, :RANK]], axis=1)
            both = jnp.concatenate([m, turned] if low_in else [turned, m], axis=0)
            parts.append(jnp.where(low64 == low_in, both, 0.0).astype(BF16))
        return jnp.concatenate(parts, axis=1)

    couplings = [coupling(k, k == 4) for k in range(6)]
    load[9].wait()
    load[10].wait()
    blank_b = jnp.zeros((RANK, RANK), BF16)
    near_coupling = jnp.concatenate(
        [m for j in range(4) for m in (ncoup_v[0, j], blank_b)], axis=1
    )
    chain = [ndown_v[0]]
    for k in range(5):
        m = sel_d[pl.ds(k, half, stride=8), :]
        down = jnp.concatenate([m[:, :RANK], m[:, RANK:]], axis=0).astype(BF16)
        chain.append(dot(chain[-1], down).astype(BF16))
    load[11].wait()
    load[12].wait()

    for i in range(2, 5):
        lc_copy(i).wait_recv()
        dens_copy(i).wait_recv()
    load[6].wait()
    load[7].wait()
    base = leaf * LEAVES - LEAVES
    for i in range(LEAVES // 2):
        far = []
        for t in (2 * i, 2 * i + 1):
            near_sum = far_sum = None
            for j in range(3):
                column = within(near_idx[j, t] - base, 0, 3 * LEAVES - 1)
                near_term = dot_nt(dens_win[column], near_v[t, j])
                near_sum = near_term if near_sum is None else near_sum + near_term
                source = within(leaf_idx[j, t] - base, 0, 3 * LEAVES - 1)
                tile = lc_win[source // 2].astype(F32)
                turned = jnp.concatenate([tile[:, RANK:], tile[:, :RANK]], axis=1)
                chosen = jnp.where(source % 2 == 1, turned, tile)[:, :RANK].astype(BF16)
                far_term = dot_nt(chosen, lcoup_v[t, j])
                far_sum = far_term if far_sum is None else far_sum + far_term
            near_own[t] = near_sum[:COLS]
            near_out[t] = near_sum[COLS:].astype(BF16)
            far.append(far_sum)
        pair = jnp.concatenate(far, axis=1)
        far_own[i] = pair[:COLS]
        far_out[i] = pair[COLS:].astype(BF16)

    swaps = [
        pltpu.make_async_remote_copy(
            src_ref=src,
            dst_ref=dst,
            send_sem=x_send.at[i],
            recv_sem=x_recv.at[i],
            device_id=partner,
            device_id_type=MESH,
        )
        for i, (src, dst) in enumerate(((near_out, near_in), (far_out, far_in)))
    ]
    for copy in swaps:
        copy.start()

    for k in range(1, PLANE):
        plane_copy(k, (group + PLANE - k) % PLANE).wait_recv()

    def source_tile(k, j):
        n = within(upper_idx[j, top // (2 << k) - 2], 64 >> k, (128 >> k) - 1)
        if k == 0:
            return tab[(n - 64) // 4, n % 4]
        if k == 1:
            return tab[(n - 32) // 2, 4 + n % 2]
        if k == 2:
            return tab[n - 16, 6]
        count = 1 << (k - 2)
        first = (n - (64 >> k)) * count
        total = None
        for i in range(count):
            part = tab[first + i, 7 if k == 3 else 8].astype(F32)
            total = part if total is None else total + part
        return total.astype(BF16)

    def node_tile(j):
        n = within(node_idx[0, j], 0, DEVS - 1)
        return tab[n // RING, n % RING]

    field = dot_nt(jnp.concatenate([node_tile(j) for j in range(4)], axis=1), near_coupling)
    for k in range(6):
        part = dot_nt(
            jnp.concatenate([source_tile(k, j) for j in range(4)], axis=1), couplings[k]
        )
        field = field + dot_nt(part.astype(BF16), chain[k])
    descended = dot_nt(field.astype(BF16), ldown_v[...].reshape(LEAVES * RANK, RANK))

    for copy in swaps:
        copy.wait_recv()
    for i in range(LEAVES // 2):
        pair = descended[:, 2 * RANK * i : 2 * RANK * (i + 1)]
        pair = pair + far_own[i] + far_in[i].astype(F32)
        stacked = jnp.concatenate(
            [jnp.where(low, pair, 0.0), jnp.where(low, 0.0, pair)], axis=0
        ).astype(BF16)
        farther = dot(stacked, rowb_v[2 * i : 2 * i + 2].reshape(2 * RANK, rowb_v.shape[2]))
        for h in range(2):
            t = 2 * i + h
            total = farther[h * COLS : (h + 1) * COLS] + near_own[t] + near_in[t].astype(F32)
            out_ref[t] = total.astype(BF16)

    for k in range(1, RING):
        ring_copy(k, z).wait_send()
    for k in range(1, PLANE):
        plane_copy(k, group).wait_send()
    for i in range(5):
        dens_copy(i).wait_send()
        lc_copy(i).wait_send()
    for copy in swaps:
        copy.wait_send()


def body(
    density,
    near_blocks,
    near_index,
    col_basis,
    row_basis,
    leaf_coupling,
    leaf_list,
    leaf_up,
    leaf_down,
    node_coupling,
    node_list,
    node_up,
    node_down,
    upper_coupling,
    upper_list,
    upper_up,
    upper_down,
):
    args = (
        jnp.swapaxes(density, 1, 2),
        near_blocks,
        near_index.T,
        jnp.swapaxes(col_basis, 1, 2),
        jnp.swapaxes(row_basis, 1, 2),
        leaf_coupling,
        leaf_list.T,
        leaf_up,
        leaf_down,
        node_coupling,
        node_list,
        node_up,
        node_down,
        jnp.transpose(upper_coupling, (1, 2, 3, 0)),
        upper_list.T,
        jnp.transpose(upper_up, (1, 2, 0)),
        jnp.transpose(upper_down, (1, 2, 0)),
    )
    held = pl.BlockSpec(memory_space=pltpu.HBM)
    small = pl.BlockSpec(memory_space=pltpu.SMEM)
    specs = [small if a.dtype == jnp.int32 else held for a in args]
    points = density.shape[1]
    dma = pltpu.SemaphoreType.DMA

    def like(i):
        return pltpu.VMEM(args[i].shape, args[i].dtype)

    result = pl.pallas_call(
        kernel,
        out_shape=pltpu.VMEM((LEAVES, COLS, points), BF16),
        in_specs=specs,
        out_specs=pl.BlockSpec(memory_space=pltpu.VMEM),
        scratch_shapes=[
            pltpu.VMEM((3 * LEAVES, 2 * COLS, points), BF16),
            like(1),
            like(3),
            like(4),
            like(5),
            like(7),
            like(8),
            like(9),
            like(11),
            like(12),
            like(13),
            like(15),
            like(16),
            pltpu.VMEM((3 * LEAVES // 2, 2 * COLS, 2 * RANK), BF16),
            pltpu.VMEM((RING, COLS, 2 * RANK), BF16),
            pltpu.VMEM((PLANE, TILES, COLS, 2 * RANK), BF16),
            pltpu.VMEM((16 * RANK // 2, 2 * RANK), F32),
            pltpu.VMEM((4, 8 * RANK // 2, 2 * RANK), F32),
            pltpu.VMEM((8 * RANK // 2, 2 * RANK), F32),
            pltpu.VMEM((LEAVES, COLS, points), F32),
            pltpu.VMEM((LEAVES, COLS, points), BF16),
            pltpu.VMEM((LEAVES, COLS, points), BF16),
            pltpu.VMEM((LEAVES // 2, COLS, 2 * RANK), F32),
            pltpu.VMEM((LEAVES // 2, COLS, 2 * RANK), BF16),
            pltpu.VMEM((LEAVES // 2, COLS, 2 * RANK), BF16),
            dma((13,)),
            dma((RING,)),
            dma((RING,)),
            dma((PLANE,)),
            dma((PLANE,)),
            dma((5,)),
            dma((5,)),
            dma((5,)),
            dma((5,)),
            dma((2,)),
            dma((2,)),
        ],
        compiler_params=pltpu.CompilerParams(
            collective_id=0, has_side_effects=True, vmem_limit_bytes=60 << 20
        ),
        name="product",
    )(*args)
    return jnp.swapaxes(result, 1, 2)


def solution(mesh):
    placed = (
        P("leaf", None, "sub"),
        P("leaf", "sub", None, None),
        P("leaf", "sub"),
        P("leaf", None, None),
        P("leaf", None, None),
        P("leaf", "sub", None, None),
        P("leaf", "sub"),
        P("leaf", None, None),
        P("leaf", None, None),
        P("leaf", None, None, None),
        P("leaf", None),
        P("leaf", None, None),
        P("leaf", None, None),
        P(),
        P(),
        P(),
        P(),
    )
    return jax.shard_map(
        body, mesh=mesh, in_specs=placed, out_specs=P("leaf", None, "sub"), check_vma=False
    )
```

```python
import jax
import jax.numpy as jnp
from jax import lax
from jax.experimental import pallas as pl
from jax.experimental.pallas import tpu as pltpu
from jax.sharding import PartitionSpec as P

MESH = pl.DeviceIdType.MESH
F32 = jnp.float32
BF16 = jnp.bfloat16

LEAVES = 8
COLS = 16
RANK = 64
RING = 8
PLANE = 16
DEVS = RING * PLANE
TILES = 5
RING_ORDER = (4, 3, 5, 2, 6, 1, 7)
PLANE_ORDER = (10, 6, 14, 9, 11, 2, 8, 5, 7, 13, 15, 1, 3, 4, 12)


def dot(a, b):
    return jnp.dot(a, b, preferred_element_type=F32)


def dot_nt(a, b):
    return lax.dot_general(a, b, (((1,), (1,)), ((), ())), preferred_element_type=F32)


def within(i, first, last):
    return jnp.minimum(jnp.maximum(i, first), last)


def kernel(
    dens_hbm,
    near_hbm,
    near_idx,
    colb_hbm,
    rowb_hbm,
    lcoup_hbm,
    leaf_idx,
    lup_hbm,
    ldown_hbm,
    ncoup_hbm,
    node_idx,
    nup_hbm,
    ndown_hbm,
    upc_hbm,
    upper_idx,
    upu_hbm,
    upd_hbm,
    out_ref,
    dens_win,
    near_v,
    colb_v,
    rowb_v,
    lcoup_v,
    lup_v,
    ldown_v,
    ncoup_v,
    nup_v,
    ndown_v,
    upc_v,
    upu_v,
    upd_v,
    lc_win,
    zbuf,
    pbuf,
    rawtab,
    tab,
    sel_up,
    sel_c,
    sel_d,
    near_own,
    near_out,
    near_in,
    far_own,
    far_out,
    far_in,
    load_sem,
    z_send,
    z_recv,
    r_send,
    r_recv,
    p_send,
    p_recv,
    q_send,
    q_recv,
    d_send,
    d_recv,
    l_send,
    l_recv,
    x_send,
    x_recv,
):
    leaf = lax.axis_index("leaf")
    sub = lax.axis_index("sub")
    other = 1 - sub
    group = leaf // RING
    z = leaf % RING
    mid = pl.ds(LEAVES, LEAVES)

    loads = [
        (dens_hbm, dens_win.at[mid, pl.ds(0, COLS), :]),
        (colb_hbm, colb_v),
        (lup_hbm, lup_v),
        (nup_hbm, nup_v),
        (upu_hbm, upu_v),
        (upc_hbm.at[pl.ds(2 * sub, 2)], upc_v),
        (near_hbm, near_v),
        (lcoup_hbm, lcoup_v),
        (upd_hbm, upd_v),
        (ndown_hbm, ndown_v),
        (ncoup_hbm, ncoup_v),
        (ldown_hbm, ldown_v),
        (rowb_hbm, rowb_v),
    ]
    load = [
        pltpu.make_async_copy(src, dst, load_sem.at[i]) for i, (src, dst) in enumerate(loads)
    ]
    for copy in load[:5]:
        copy.start()

    def ring_peer(k):
        return {"leaf": group * RING + (z + k) % RING, "sub": sub}

    def plane_peer(k):
        return {"leaf": ((group + k) % PLANE) * RING + z, "sub": sub}

    after, before = (leaf + 1) % DEVS, (leaf + DEVS - 1) % DEVS
    partner = {"leaf": leaf, "sub": other}
    moves = [
        ({"leaf": after, "sub": sub}, LEAVES, 0, 0),
        ({"leaf": before, "sub": sub}, LEAVES, 2 * LEAVES, 0),
        (partner, LEAVES, LEAVES, COLS),
        (partner, 0, 0, COLS),
        (partner, 2 * LEAVES, 2 * LEAVES, COLS),
    ]

    barrier = pltpu.get_barrier_semaphore()
    greeted = (
        [ring_peer(k) for k in RING_ORDER]
        + [plane_peer(k) for k in PLANE_ORDER]
        + [device for device, _, _, _ in moves[:3]]
    )
    for device in greeted:
        pl.semaphore_signal(barrier, inc=1, device_id=device, device_id_type=MESH)

    load[0].wait()
    load[1].wait()
    pairs = []
    for i in range(LEAVES // 2):
        halves = [
            dot_nt(dens_win[LEAVES + t, 0:COLS, :], colb_v[t]) for t in (2 * i, 2 * i + 1)
        ]
        pair = jnp.concatenate(halves, axis=1).astype(BF16)
        lc_win[LEAVES // 2 + i, 0:COLS, :] = pair
        pairs.append(pair)
    load[2].wait()
    load[3].wait()
    for copy in load[5:]:
        copy.start()
    raw = dot(jnp.concatenate(pairs, axis=1), lup_v[...].reshape(LEAVES * RANK, RANK))
    raised = dot(raw.astype(BF16), nup_v[0])
    tile = jnp.concatenate([raw, raised], axis=1).astype(BF16)
    zbuf[z] = tile
    pbuf[group] = tile

    def one_hot(target, count):
        column = lax.broadcasted_iota(jnp.int32, (target.shape[0], count), 1)
        return (column == target).astype(F32).astype(BF16)

    row16 = lax.broadcasted_iota(jnp.int32, (16, 1), 0)
    target = jnp.where(
        row16 < 4,
        60 + 4 * group + row16,
        jnp.where(
            row16 < 6,
            24 + 2 * group + row16,
            jnp.where(row16 == 6, 12 + group, jnp.where(row16 == 7, 4 + group // 2, group // 4)),
        ),
    )
    pick_up = one_hot(target, upu_v.shape[2])
    half = RANK // 2

    def extract(pick, source, dest, rows):
        def step(r, carry):
            slab = jnp.concatenate([source[r], source[r + half]], axis=0)
            dest[pl.ds(pl.multiple_of(r * rows, rows), rows), :] = dot_nt(pick, slab)
            return carry

        lax.fori_loop(0, half, step, 0, unroll=8)

    load[4].wait()
    extract(pick_up, upu_v, sel_up, 16)

    def matrix_up(k):
        m = sel_up[pl.ds(k, half, stride=16), :]
        return jnp.concatenate([m[:, :RANK], m[:, RANK:]], axis=0)

    blank = jnp.zeros((RANK, RANK), F32)
    up = []
    for k in range(4):
        wide = [matrix_up(k), blank] if k < 2 else [blank, matrix_up(k)]
        up += [jnp.zeros((RANK, 2 * RANK), F32), jnp.concatenate(wide, axis=1)]
    first = jnp.concatenate(up, axis=0).astype(BF16)
    second = [jnp.concatenate([matrix_up(4), matrix_up(5)], axis=0)]
    for k in (6, 7, 8):
        second.append(dot(second[-1].astype(BF16), matrix_up(k).astype(BF16)))
    second = jnp.concatenate(second, axis=1).astype(BF16)
    up = jnp.concatenate([first, dot(first, second).astype(BF16)], axis=1)

    pl.semaphore_wait(barrier, len(greeted))

    def ring_copy(k, slot):
        return pltpu.make_async_remote_copy(
            src_ref=zbuf.at[slot],
            dst_ref=zbuf.at[slot],
            send_sem=z_send.at[k],
            recv_sem=z_recv.at[k],
            device_id=ring_peer(k),
            device_id_type=MESH,
        )

    for k in RING_ORDER:
        ring_copy(k, z).start()

    def raw_copy(k, slot):
        return pltpu.make_async_remote_copy(
            src_ref=pbuf.at[slot],
            dst_ref=pbuf.at[slot],
            send_sem=r_send.at[k],
            recv_sem=r_recv.at[k],
            device_id=plane_peer(k),
            device_id_type=MESH,
        )

    for k in PLANE_ORDER:
        raw_copy(k, group).start()

    def dens_copy(i):
        device, here, there, row = moves[i]
        return pltpu.make_async_remote_copy(
            src_ref=dens_win.at[pl.ds(here, LEAVES), pl.ds(0, COLS), :],
            dst_ref=dens_win.at[pl.ds(there, LEAVES), pl.ds(row, COLS), :],
            send_sem=d_send.at[i],
            recv_sem=d_recv.at[i],
            device_id=device,
            device_id_type=MESH,
        )

    def lc_copy(i):
        device, here, there, row = moves[i]
        return pltpu.make_async_remote_copy(
            src_ref=lc_win.at[pl.ds(here // 2, LEAVES // 2), pl.ds(0, COLS), :],
            dst_ref=lc_win.at[pl.ds(there // 2, LEAVES // 2), pl.ds(row, COLS), :],
            send_sem=l_send.at[i],
            recv_sem=l_recv.at[i],
            device_id=device,
            device_id_type=MESH,
        )

    for i in range(3):
        lc_copy(i).start()
        dens_copy(i).start()

    row8 = lax.broadcasted_iota(jnp.int32, (8, 1), 0)
    top = DEVS + leaf
    node_of = jnp.zeros((8, 1), jnp.int32)
    for k in range(6):
        node_of = jnp.where(row8 == k, top // (2 << k), node_of)
    load[5].wait()
    load[8].wait()
    pick_c = one_hot(node_of - 2, upc_v.shape[3])
    pick_d = one_hot(node_of - 4, upd_v.shape[2])
    for j in range(2):
        extract(pick_c, upc_v.at[j], sel_c.at[2 * sub + j], 8)
    share = pltpu.make_async_remote_copy(
        src_ref=sel_c.at[pl.ds(2 * sub, 2)],
        dst_ref=sel_c.at[pl.ds(2 * sub, 2)],
        send_sem=x_send.at[2],
        recv_sem=x_recv.at[2],
        device_id=partner,
        device_id_type=MESH,
    )
    share.start()
    extract(pick_d, upd_v, sel_d, 8)

    load[9].wait()
    chain = [ndown_v[0]]
    for k in range(5):
        m = sel_d[pl.ds(k, half, stride=8), :]
        down = jnp.concatenate([m[:, :RANK], m[:, RANK:]], axis=0).astype(BF16)
        chain.append(dot(chain[-1], down).astype(BF16))
    load[11].wait()
    load[12].wait()

    for k in range(1, PLANE):
        raw_copy(k, (group + PLANE - k) % PLANE).wait_recv()
    low = lax.broadcasted_iota(jnp.int32, (COLS, 2 * RANK), 1) < RANK

    def turn(m):
        return jnp.concatenate([m[:, RANK:], m[:, :RANK]], axis=1)

    for i in range(PLANE // 2):
        rawtab[z, i] = jnp.where(
            low, pbuf[2 * i].astype(F32), turn(pbuf[2 * i + 1].astype(F32))
        ).astype(BF16)

    def along_copy(k, slot):
        return pltpu.make_async_remote_copy(
            src_ref=rawtab.at[slot],
            dst_ref=rawtab.at[slot],
            send_sem=q_send.at[k],
            recv_sem=q_recv.at[k],
            device_id=ring_peer(k),
            device_id_type=MESH,
        )

    for k in RING_ORDER:
        along_copy(k, z).start()

    for k in range(1, RING):
        ring_copy(k, (z + RING - k) % RING).wait_recv()
    c64 = [zbuf[2 * i].astype(F32) + zbuf[2 * i + 1].astype(F32) for i in range(4)]
    sums = dot(jnp.concatenate([c.astype(BF16) for c in c64], axis=1), up)
    tab[group, 0] = jnp.where(low, turn(c64[0]), c64[1]).astype(BF16)
    tab[group, 1] = jnp.where(low, turn(c64[2]), c64[3]).astype(BF16)
    for i in range(3):
        tab[group, 2 + i] = sums[:, 2 * RANK * i : 2 * RANK * (i + 1)].astype(BF16)

    def plane_copy(k, slot):
        return pltpu.make_async_remote_copy(
            src_ref=tab.at[slot],
            dst_ref=tab.at[slot],
            send_sem=p_send.at[k],
            recv_sem=p_recv.at[k],
            device_id=plane_peer(k),
            device_id_type=MESH,
        )

    for k in PLANE_ORDER:
        plane_copy(k, group).start()
    for i in range(2):
        lc_copy(i).wait_recv()
        lc_copy(3 + i).start()
        dens_copy(i).wait_recv()
        dens_copy(3 + i).start()

    low64 = lax.broadcasted_iota(jnp.int32, (half, 2 * RANK), 1) < RANK

    def coupling(k):
        parts = []
        for j in range(4):
            m = sel_c[j, pl.ds(k, half, stride=8), :]
            turned = jnp.concatenate([m[:, RANK:], m[:, :RANK]], axis=1)
            both = [jnp.where(low64, m, turned), jnp.where(low64, turned, m)]
            parts.append(jnp.concatenate(both, axis=0).astype(BF16))
        return jnp.concatenate(parts, axis=1)

    pltpu.make_async_remote_copy(
        src_ref=sel_c.at[pl.ds(2 * other, 2)],
        dst_ref=sel_c.at[pl.ds(2 * other, 2)],
        send_sem=x_send.at[2],
        recv_sem=x_recv.at[2],
        device_id=partner,
        device_id_type=MESH,
    ).wait_recv()
    couplings = [coupling(k) for k in range(6)]
    load[10].wait()
    near_coupling = jnp.concatenate([ncoup_v[0, j // 2] for j in range(8)], axis=1)
    for i in range(2, 5):
        lc_copy(i).wait_recv()
        dens_copy(i).wait_recv()
    load[6].wait()
    load[7].wait()
    base = leaf * LEAVES - LEAVES
    for i in range(LEAVES // 2):
        far = []
        for t in (2 * i, 2 * i + 1):
            near_sum = far_sum = None
            for j in range(3):
                column = within(near_idx[j, t] - base, 0, 3 * LEAVES - 1)
                near_term = dot_nt(dens_win[column], near_v[t, j])
                near_sum = near_term if near_sum is None else near_sum + near_term
                source = within(leaf_idx[j, t] - base, 0, 3 * LEAVES - 1)
                tile = lc_win[source // 2].astype(F32)
                turned = jnp.concatenate([tile[:, RANK:], tile[:, :RANK]], axis=1)
                chosen = jnp.where(source % 2 == 1, turned, tile)[:, :RANK].astype(BF16)
                far_term = dot_nt(chosen, lcoup_v[t, j])
                far_sum = far_term if far_sum is None else far_sum + far_term
            near_own[t] = near_sum[:COLS]
            near_out[t] = near_sum[COLS:].astype(BF16)
            far.append(far_sum)
        pair = jnp.concatenate(far, axis=1)
        far_own[i] = pair[:COLS]
        far_out[i] = pair[COLS:].astype(BF16)

    swaps = [
        pltpu.make_async_remote_copy(
            src_ref=src,
            dst_ref=dst,
            send_sem=x_send.at[i],
            recv_sem=x_recv.at[i],
            device_id=partner,
            device_id_type=MESH,
        )
        for i, (src, dst) in enumerate(((near_out, near_in), (far_out, far_in)))
    ]
    for copy in swaps:
        copy.start()

    for k in range(1, PLANE):
        plane_copy(k, (group + PLANE - k) % PLANE).wait_recv()

    def source_tile(k, j):
        n = within(upper_idx[j, top // (2 << k) - 2], 64 >> k, (128 >> k) - 1)
        if k < 3:
            place = (n - 64) // 4, n % 4 // 2
            if k == 1:
                place = (n - 32) // 2, 2
            if k == 2:
                place = n - 16, 3
            total = tab[place[0], place[1]].astype(F32)
            return jnp.where(low == (n % 2 == 0 if k < 2 else True), total, 0.0).astype(BF16)
        count = 1 << (k - 2)
        first = (n - (64 >> k)) * count
        total = None
        for i in range(count):
            part = tab[first + i, 3 if k == 3 else 4].astype(F32)
            total = part if total is None else total + part
        return jnp.where(low == (k == 4), total, 0.0).astype(BF16)

    def node_tile(j):
        n = within(node_idx[0, j], 0, DEVS - 1)
        tile = rawtab[n % RING, n // (2 * RING)].astype(F32)
        return jnp.where(low == (n // RING % 2 == 0), tile, 0.0).astype(BF16)

    field = None
    for k in range(6):
        part = dot_nt(
            jnp.concatenate([source_tile(k, j) for j in range(4)], axis=1), couplings[k]
        )
        part = dot_nt(part.astype(BF16), chain[k])
        field = part if field is None else field + part
    for k in range(1, RING):
        along_copy(k, (z + RING - k) % RING).wait_recv()
    field = field + dot_nt(
        jnp.concatenate([node_tile(j) for j in range(4)], axis=1), near_coupling
    )
    descended = dot_nt(field.astype(BF16), ldown_v[...].reshape(LEAVES * RANK, RANK))

    for copy in swaps:
        copy.wait_recv()
    for i in range(LEAVES // 2):
        pair = descended[:, 2 * RANK * i : 2 * RANK * (i + 1)]
        pair = pair + far_own[i] + far_in[i].astype(F32)
        stacked = jnp.concatenate(
            [jnp.where(low, pair, 0.0), jnp.where(low, 0.0, pair)], axis=0
        ).astype(BF16)
        farther = dot(stacked, rowb_v[2 * i : 2 * i + 2].reshape(2 * RANK, rowb_v.shape[2]))
        for h in range(2):
            t = 2 * i + h
            total = farther[h * COLS : (h + 1) * COLS] + near_own[t] + near_in[t].astype(F32)
            out_ref[t] = total.astype(BF16)

    for k in range(1, RING):
        ring_copy(k, z).wait_send()
        along_copy(k, z).wait_send()
    for k in range(1, PLANE):
        raw_copy(k, group).wait_send()
        plane_copy(k, group).wait_send()
    for i in range(5):
        dens_copy(i).wait_send()
        lc_copy(i).wait_send()
    for copy in swaps + [share]:
        copy.wait_send()


def body(
    density,
    near_blocks,
    near_index,
    col_basis,
    row_basis,
    leaf_coupling,
    leaf_list,
    leaf_up,
    leaf_down,
    node_coupling,
    node_list,
    node_up,
    node_down,
    upper_coupling,
    upper_list,
    upper_up,
    upper_down,
):
    args = (
        jnp.swapaxes(density, 1, 2),
        near_blocks,
        near_index.T,
        jnp.swapaxes(col_basis, 1, 2),
        jnp.swapaxes(row_basis, 1, 2),
        leaf_coupling,
        leaf_list.T,
        leaf_up,
        leaf_down,
        node_coupling,
        node_list,
        node_up,
        node_down,
        jnp.transpose(upper_coupling, (1, 2, 3, 0)),
        upper_list.T,
        jnp.transpose(upper_up, (1, 2, 0)),
        jnp.transpose(upper_down, (1, 2, 0)),
    )
    held = pl.BlockSpec(memory_space=pltpu.HBM)
    small = pl.BlockSpec(memory_space=pltpu.SMEM)
    specs = [small if a.dtype == jnp.int32 else held for a in args]
    points = density.shape[1]
    dma = pltpu.SemaphoreType.DMA

    def like(i):
        return pltpu.VMEM(args[i].shape, args[i].dtype)

    result = pl.pallas_call(
        kernel,
        out_shape=pltpu.VMEM((LEAVES, COLS, points), BF16),
        in_specs=specs,
        out_specs=pl.BlockSpec(memory_space=pltpu.VMEM),
        scratch_shapes=[
            pltpu.VMEM((3 * LEAVES, 2 * COLS, points), BF16),
            like(1),
            like(3),
            like(4),
            like(5),
            like(7),
            like(8),
            like(9),
            like(11),
            like(12),
            pltpu.VMEM((2,) + args[13].shape[1:], BF16),
            like(15),
            like(16),
            pltpu.VMEM((3 * LEAVES // 2, 2 * COLS, 2 * RANK), BF16),
            pltpu.VMEM((RING, COLS, 2 * RANK), BF16),
            pltpu.VMEM((PLANE, COLS, 2 * RANK), BF16),
            pltpu.VMEM((RING, PLANE // 2, COLS, 2 * RANK), BF16),
            pltpu.VMEM((PLANE, TILES, COLS, 2 * RANK), BF16),
            pltpu.VMEM((16 * RANK // 2, 2 * RANK), F32),
            pltpu.VMEM((4, 8 * RANK // 2, 2 * RANK), F32),
            pltpu.VMEM((8 * RANK // 2, 2 * RANK), F32),
            pltpu.VMEM((LEAVES, COLS, points), F32),
            pltpu.VMEM((LEAVES, COLS, points), BF16),
            pltpu.VMEM((LEAVES, COLS, points), BF16),
            pltpu.VMEM((LEAVES // 2, COLS, 2 * RANK), F32),
            pltpu.VMEM((LEAVES // 2, COLS, 2 * RANK), BF16),
            pltpu.VMEM((LEAVES // 2, COLS, 2 * RANK), BF16),
            dma((13,)),
            dma((RING,)),
            dma((RING,)),
            dma((PLANE,)),
            dma((PLANE,)),
            dma((PLANE,)),
            dma((PLANE,)),
            dma((RING,)),
            dma((RING,)),
            dma((5,)),
            dma((5,)),
            dma((5,)),
            dma((5,)),
            dma((3,)),
            dma((3,)),
        ],
        compiler_params=pltpu.CompilerParams(
            collective_id=0, has_side_effects=True, vmem_limit_bytes=60 << 20
        ),
        name="product",
    )(*args)
    return jnp.swapaxes(result, 1, 2)


def solution(mesh):
    placed = (
        P("leaf", None, "sub"),
        P("leaf", "sub", None, None),
        P("leaf", "sub"),
        P("leaf", None, None),
        P("leaf", None, None),
        P("leaf", "sub", None, None),
        P("leaf", "sub"),
        P("leaf", None, None),
        P("leaf", None, None),
        P("leaf", None, None, None),
        P("leaf", None),
        P("leaf", None, None),
        P("leaf", None, None),
        P(),
        P(),
        P(),
        P(),
    )
    return jax.shard_map(
        body, mesh=mesh, in_specs=placed, out_specs=P("leaf", None, "sub"), check_vma=False
    )
```

```python
import jax
import jax.numpy as jnp
from jax import lax
from jax.experimental import pallas as pl
from jax.experimental.pallas import tpu as pltpu
from jax.sharding import PartitionSpec as P

MESH = pl.DeviceIdType.MESH
F32 = jnp.float32
BF16 = jnp.bfloat16

LEAVES = 8
COLS = 16
RANK = 64
RING = 8
PLANE = 16
DEVS = RING * PLANE
TILES = 5
RING_ORDER = (4, 3, 5, 2, 6, 1, 7)
PLANE_ORDER = (10, 6, 14, 9, 11, 2, 8, 5, 7, 13, 15, 1, 3, 4, 12)


def dot(a, b):
    return jnp.dot(a, b, preferred_element_type=F32)


def dot_nt(a, b):
    return lax.dot_general(a, b, (((1,), (1,)), ((), ())), preferred_element_type=F32)


def within(i, first, last):
    return jnp.minimum(jnp.maximum(i, first), last)


def kernel(
    dens_hbm,
    near_hbm,
    near_idx,
    colb_hbm,
    rowb_hbm,
    lcoup_hbm,
    leaf_idx,
    lup_hbm,
    ldown_hbm,
    ncoup_hbm,
    node_idx,
    nup_hbm,
    ndown_hbm,
    upc_hbm,
    upper_idx,
    upu_hbm,
    upd_hbm,
    out_ref,
    dens_win,
    near_v,
    colb_v,
    rowb_v,
    lcoup_v,
    lup_v,
    ldown_v,
    ncoup_v,
    nup_v,
    ndown_v,
    upc_v,
    upu_v,
    upd_v,
    lc_win,
    zbuf,
    pbuf,
    rawtab,
    tab,
    sel_up,
    sel_c,
    sel_d,
    near_own,
    near_out,
    near_in,
    far_own,
    far_out,
    far_in,
    load_sem,
    z_send,
    z_recv,
    r_send,
    r_recv,
    p_send,
    p_recv,
    q_send,
    q_recv,
    d_send,
    d_recv,
    l_send,
    l_recv,
    x_send,
    x_recv,
):
    leaf = lax.axis_index("leaf")
    sub = lax.axis_index("sub")
    other = 1 - sub
    group = leaf // RING
    z = leaf % RING
    mid = pl.ds(LEAVES, LEAVES)

    loads = [
        (dens_hbm, dens_win.at[mid, pl.ds(0, COLS), :]),
        (colb_hbm, colb_v),
        (lup_hbm, lup_v),
        (nup_hbm, nup_v),
        (upu_hbm, upu_v),
        (upc_hbm, upc_v),
        (near_hbm, near_v),
        (lcoup_hbm, lcoup_v),
        (upd_hbm, upd_v),
        (ndown_hbm, ndown_v),
        (ncoup_hbm, ncoup_v),
        (ldown_hbm, ldown_v),
        (rowb_hbm, rowb_v),
    ]
    load = [
        pltpu.make_async_copy(src, dst, load_sem.at[i]) for i, (src, dst) in enumerate(loads)
    ]
    for copy in load[:5]:
        copy.start()

    def ring_peer(k):
        return {"leaf": group * RING + (z + k) % RING, "sub": sub}

    def plane_peer(k):
        return {"leaf": ((group + k) % PLANE) * RING + z, "sub": sub}

    after, before = (leaf + 1) % DEVS, (leaf + DEVS - 1) % DEVS
    partner = {"leaf": leaf, "sub": other}
    moves = [
        ({"leaf": after, "sub": sub}, LEAVES, 0, 0),
        ({"leaf": before, "sub": sub}, LEAVES, 2 * LEAVES, 0),
        (partner, LEAVES, LEAVES, COLS),
        (partner, 0, 0, COLS),
        (partner, 2 * LEAVES, 2 * LEAVES, COLS),
    ]

    barrier = pltpu.get_barrier_semaphore()
    greeted = (
        [ring_peer(k) for k in RING_ORDER]
        + [plane_peer(k) for k in PLANE_ORDER]
        + [device for device, _, _, _ in moves[:3]]
    )
    for device in greeted:
        pl.semaphore_signal(barrier, inc=1, device_id=device, device_id_type=MESH)

    load[0].wait()
    load[1].wait()
    pairs = []
    for i in range(LEAVES // 2):
        halves = [
            dot_nt(dens_win[LEAVES + t, 0:COLS, :], colb_v[t]) for t in (2 * i, 2 * i + 1)
        ]
        pair = jnp.concatenate(halves, axis=1).astype(BF16)
        lc_win[LEAVES // 2 + i, 0:COLS, :] = pair
        pairs.append(pair)
    load[2].wait()
    load[3].wait()
    for copy in load[5:]:
        copy.start()
    raw = dot(jnp.concatenate(pairs, axis=1), lup_v[...].reshape(LEAVES * RANK, RANK))
    raised = dot(raw.astype(BF16), nup_v[0])
    tile = jnp.concatenate([raw, raised], axis=1).astype(BF16)
    zbuf[z] = tile
    pbuf[group] = tile

    def one_hot(target, count):
        column = lax.broadcasted_iota(jnp.int32, (target.shape[0], count), 1)
        return (column == target).astype(F32).astype(BF16)

    row16 = lax.broadcasted_iota(jnp.int32, (16, 1), 0)
    target = jnp.where(
        row16 < 4,
        60 + 4 * group + row16,
        jnp.where(
            row16 < 6,
            24 + 2 * group + row16,
            jnp.where(row16 == 6, 12 + group, jnp.where(row16 == 7, 4 + group // 2, group // 4)),
        ),
    )
    pick_up = one_hot(target, upu_v.shape[2])
    half = RANK // 2

    def extract(pick, source, dest, rows):
        for r in range(0, half, 2):
            slabs = [source[i] for i in (r, r + half, r + 1, r + 1 + half)]
            both = dot_nt(pick, jnp.concatenate(slabs, axis=0))
            for a in range(2):
                first = (r + a) * rows
                dest[first : first + rows, :] = both[:, 2 * RANK * a : 2 * RANK * (a + 1)]

    load[4].wait()
    extract(pick_up, upu_v, sel_up, 16)

    def matrix_up(k):
        m = sel_up[pl.ds(k, half, stride=16), :]
        return jnp.concatenate([m[:, :RANK], m[:, RANK:]], axis=0)

    blank = jnp.zeros((RANK, RANK), F32)
    up = []
    for k in range(4):
        wide = [matrix_up(k), blank] if k < 2 else [blank, matrix_up(k)]
        up += [jnp.zeros((RANK, 2 * RANK), F32), jnp.concatenate(wide, axis=1)]
    first = jnp.concatenate(up, axis=0).astype(BF16)
    second = [jnp.concatenate([matrix_up(4), matrix_up(5)], axis=0)]
    for k in (6, 7, 8):
        second.append(dot(second[-1].astype(BF16), matrix_up(k).astype(BF16)))
    second = jnp.concatenate(second, axis=1).astype(BF16)
    up = jnp.concatenate([first, dot(first, second).astype(BF16)], axis=1)

    pl.semaphore_wait(barrier, len(greeted))

    def ring_copy(k, slot):
        return pltpu.make_async_remote_copy(
            src_ref=zbuf.at[slot],
            dst_ref=zbuf.at[slot],
            send_sem=z_send.at[k],
            recv_sem=z_recv.at[k],
            device_id=ring_peer(k),
            device_id_type=MESH,
        )

    for k in RING_ORDER:
        ring_copy(k, z).start()

    def raw_copy(k, slot):
        return pltpu.make_async_remote_copy(
            src_ref=pbuf.at[slot],
            dst_ref=pbuf.at[slot],
            send_sem=r_send.at[k],
            recv_sem=r_recv.at[k],
            device_id=plane_peer(k),
            device_id_type=MESH,
        )

    def dens_copy(i):
        device, here, there, row = moves[i]
        return pltpu.make_async_remote_copy(
            src_ref=dens_win.at[pl.ds(here, LEAVES), pl.ds(0, COLS), :],
            dst_ref=dens_win.at[pl.ds(there, LEAVES), pl.ds(row, COLS), :],
            send_sem=d_send.at[i],
            recv_sem=d_recv.at[i],
            device_id=device,
            device_id_type=MESH,
        )

    def lc_copy(i):
        device, here, there, row = moves[i]
        return pltpu.make_async_remote_copy(
            src_ref=lc_win.at[pl.ds(here // 2, LEAVES // 2), pl.ds(0, COLS), :],
            dst_ref=lc_win.at[pl.ds(there // 2, LEAVES // 2), pl.ds(row, COLS), :],
            send_sem=l_send.at[i],
            recv_sem=l_recv.at[i],
            device_id=device,
            device_id_type=MESH,
        )

    for i in range(3):
        lc_copy(i).start()
        dens_copy(i).start()
    for k in PLANE_ORDER:
        raw_copy(k, group).start()

    row8 = lax.broadcasted_iota(jnp.int32, (8, 1), 0)
    top = DEVS + leaf
    node_of = jnp.zeros((8, 1), jnp.int32)
    for k in range(6):
        node_of = jnp.where(row8 == k, top // (2 << k), node_of)
    load[5].wait()
    load[8].wait()
    pick_c = one_hot(node_of - 2, upc_v.shape[3])
    pick_d = one_hot(node_of - 4, upd_v.shape[2])
    for j in range(4):
        extract(pick_c, upc_v.at[j], sel_c.at[j], 8)
    extract(pick_d, upd_v, sel_d, 8)

    load[9].wait()
    chain = [ndown_v[0]]
    for k in range(5):
        m = sel_d[pl.ds(k, half, stride=8), :]
        down = jnp.concatenate([m[:, :RANK], m[:, RANK:]], axis=0).astype(BF16)
        chain.append(dot(chain[-1], down).astype(BF16))
    load[11].wait()
    load[12].wait()

    low = lax.broadcasted_iota(jnp.int32, (COLS, 2 * RANK), 1) < RANK

    def turn(m):
        return jnp.concatenate([m[:, RANK:], m[:, :RANK]], axis=1)

    for k in range(1, RING):
        ring_copy(k, (z + RING - k) % RING).wait_recv()
    c64 = [zbuf[2 * i].astype(F32) + zbuf[2 * i + 1].astype(F32) for i in range(4)]
    sums = dot(jnp.concatenate([c.astype(BF16) for c in c64], axis=1), up)
    tab[group, 0] = jnp.where(low, turn(c64[0]), c64[1]).astype(BF16)
    tab[group, 1] = jnp.where(low, turn(c64[2]), c64[3]).astype(BF16)
    for i in range(3):
        tab[group, 2 + i] = sums[:, 2 * RANK * i : 2 * RANK * (i + 1)].astype(BF16)

    def plane_copy(k, slot):
        return pltpu.make_async_remote_copy(
            src_ref=tab.at[slot],
            dst_ref=tab.at[slot],
            send_sem=p_send.at[k],
            recv_sem=p_recv.at[k],
            device_id=plane_peer(k),
            device_id_type=MESH,
        )

    for k in PLANE_ORDER:
        plane_copy(k, group).start()
    for k in range(1, PLANE):
        raw_copy(k, (group + PLANE - k) % PLANE).wait_recv()
    for i in range(PLANE // 2):
        rawtab[z, i] = jnp.where(
            low, pbuf[2 * i].astype(F32), turn(pbuf[2 * i + 1].astype(F32))
        ).astype(BF16)

    def along_copy(k, slot):
        return pltpu.make_async_remote_copy(
            src_ref=rawtab.at[slot],
            dst_ref=rawtab.at[slot],
            send_sem=q_send.at[k],
            recv_sem=q_recv.at[k],
            device_id=ring_peer(k),
            device_id_type=MESH,
        )

    for k in RING_ORDER:
        along_copy(k, z).start()

    for i in range(2):
        lc_copy(i).wait_recv()
        lc_copy(3 + i).start()
        dens_copy(i).wait_recv()
        dens_copy(3 + i).start()

    low64 = lax.broadcasted_iota(jnp.int32, (half, 2 * RANK), 1) < RANK

    def coupling(k):
        parts = []
        for j in range(4):
            m = sel_c[j, pl.ds(k, half, stride=8), :]
            turned = jnp.concatenate([m[:, RANK:], m[:, :RANK]], axis=1)
            both = [jnp.where(low64, m, turned), jnp.where(low64, turned, m)]
            parts.append(jnp.concatenate(both, axis=0).astype(BF16))
        return jnp.concatenate(parts, axis=1)

    couplings = [coupling(k) for k in range(6)]
    load[10].wait()
    near_coupling = jnp.concatenate([ncoup_v[0, j // 2] for j in range(8)], axis=1)
    for i in range(2, 5):
        lc_copy(i).wait_recv()
        dens_copy(i).wait_recv()
    load[6].wait()
    load[7].wait()
    base = leaf * LEAVES - LEAVES
    for i in range(LEAVES // 2):
        far = []
        for t in (2 * i, 2 * i + 1):
            near_sum = far_sum = None
            for j in range(3):
                column = within(near_idx[j, t] - base, 0, 3 * LEAVES - 1)
                near_term = dot_nt(dens_win[column], near_v[t, j])
                near_sum = near_term if near_sum is None else near_sum + near_term
                source = within(leaf_idx[j, t] - base, 0, 3 * LEAVES - 1)
                tile = lc_win[source // 2].astype(F32)
                turned = jnp.concatenate([tile[:, RANK:], tile[:, :RANK]], axis=1)
                chosen = jnp.where(source % 2 == 1, turned, tile)[:, :RANK].astype(BF16)
                far_term = dot_nt(chosen, lcoup_v[t, j])
                far_sum = far_term if far_sum is None else far_sum + far_term
            near_own[t] = near_sum[:COLS]
            near_out[t] = near_sum[COLS:].astype(BF16)
            far.append(far_sum)
        pair = jnp.concatenate(far, axis=1)
        far_own[i] = pair[:COLS]
        far_out[i] = pair[COLS:].astype(BF16)

    swaps = [
        pltpu.make_async_remote_copy(
            src_ref=src,
            dst_ref=dst,
            send_sem=x_send.at[i],
            recv_sem=x_recv.at[i],
            device_id=partner,
            device_id_type=MESH,
        )
        for i, (src, dst) in enumerate(((near_out, near_in), (far_out, far_in)))
    ]
    for copy in swaps:
        copy.start()

    for k in range(1, PLANE):
        plane_copy(k, (group + PLANE - k) % PLANE).wait_recv()

    def source_tile(k, j):
        n = within(upper_idx[j, top // (2 << k) - 2], 64 >> k, (128 >> k) - 1)
        if k < 3:
            place = (n - 64) // 4, n % 4 // 2
            if k == 1:
                place = (n - 32) // 2, 2
            if k == 2:
                place = n - 16, 3
            total = tab[place[0], place[1]].astype(F32)
            return jnp.where(low == (n % 2 == 0 if k < 2 else True), total, 0.0).astype(BF16)
        count = 1 << (k - 2)
        first = (n - (64 >> k)) * count
        total = None
        for i in range(count):
            part = tab[first + i, 3 if k == 3 else 4].astype(F32)
            total = part if total is None else total + part
        return jnp.where(low == (k == 4), total, 0.0).astype(BF16)

    def node_tile(j):
        n = within(node_idx[0, j], 0, DEVS - 1)
        tile = rawtab[n % RING, n // (2 * RING)].astype(F32)
        return jnp.where(low == (n // RING % 2 == 0), tile, 0.0).astype(BF16)

    field = None
    for k in range(6):
        part = dot_nt(
            jnp.concatenate([source_tile(k, j) for j in range(4)], axis=1), couplings[k]
        )
        part = dot_nt(part.astype(BF16), chain[k])
        field = part if field is None else field + part
    for k in range(1, RING):
        along_copy(k, (z + RING - k) % RING).wait_recv()
    field = field + dot_nt(
        jnp.concatenate([node_tile(j) for j in range(4)], axis=1), near_coupling
    )
    descended = dot_nt(field.astype(BF16), ldown_v[...].reshape(LEAVES * RANK, RANK))

    for copy in swaps:
        copy.wait_recv()
    for i in range(LEAVES // 2):
        pair = descended[:, 2 * RANK * i : 2 * RANK * (i + 1)]
        pair = pair + far_own[i] + far_in[i].astype(F32)
        stacked = jnp.concatenate(
            [jnp.where(low, pair, 0.0), jnp.where(low, 0.0, pair)], axis=0
        ).astype(BF16)
        farther = dot(stacked, rowb_v[2 * i : 2 * i + 2].reshape(2 * RANK, rowb_v.shape[2]))
        for h in range(2):
            t = 2 * i + h
            total = farther[h * COLS : (h + 1) * COLS] + near_own[t] + near_in[t].astype(F32)
            out_ref[t] = total.astype(BF16)

    for k in range(1, RING):
        ring_copy(k, z).wait_send()
        along_copy(k, z).wait_send()
    for k in range(1, PLANE):
        raw_copy(k, group).wait_send()
        plane_copy(k, group).wait_send()
    for i in range(5):
        dens_copy(i).wait_send()
        lc_copy(i).wait_send()
    for copy in swaps:
        copy.wait_send()


def body(
    density,
    near_blocks,
    near_index,
    col_basis,
    row_basis,
    leaf_coupling,
    leaf_list,
    leaf_up,
    leaf_down,
    node_coupling,
    node_list,
    node_up,
    node_down,
    upper_coupling,
    upper_list,
    upper_up,
    upper_down,
):
    args = (
        jnp.swapaxes(density, 1, 2),
        near_blocks,
        near_index.T,
        jnp.swapaxes(col_basis, 1, 2),
        jnp.swapaxes(row_basis, 1, 2),
        leaf_coupling,
        leaf_list.T,
        leaf_up,
        leaf_down,
        node_coupling,
        node_list,
        node_up,
        node_down,
        jnp.transpose(upper_coupling, (1, 2, 3, 0)),
        upper_list.T,
        jnp.transpose(upper_up, (1, 2, 0)),
        jnp.transpose(upper_down, (1, 2, 0)),
    )
    held = pl.BlockSpec(memory_space=pltpu.HBM)
    small = pl.BlockSpec(memory_space=pltpu.SMEM)
    specs = [small if a.dtype == jnp.int32 else held for a in args]
    points = density.shape[1]
    dma = pltpu.SemaphoreType.DMA

    def like(i):
        return pltpu.VMEM(args[i].shape, args[i].dtype)

    result = pl.pallas_call(
        kernel,
        out_shape=pltpu.VMEM((LEAVES, COLS, points), BF16),
        in_specs=specs,
        out_specs=pl.BlockSpec(memory_space=pltpu.VMEM),
        scratch_shapes=[
            pltpu.VMEM((3 * LEAVES, 2 * COLS, points), BF16),
            like(1),
            like(3),
            like(4),
            like(5),
            like(7),
            like(8),
            like(9),
            like(11),
            like(12),
            like(13),
            like(15),
            like(16),
            pltpu.VMEM((3 * LEAVES // 2, 2 * COLS, 2 * RANK), BF16),
            pltpu.VMEM((RING, COLS, 2 * RANK), BF16),
            pltpu.VMEM((PLANE, COLS, 2 * RANK), BF16),
            pltpu.VMEM((RING, PLANE // 2, COLS, 2 * RANK), BF16),
            pltpu.VMEM((PLANE, TILES, COLS, 2 * RANK), BF16),
            pltpu.VMEM((16 * RANK // 2, 2 * RANK), F32),
            pltpu.VMEM((4, 8 * RANK // 2, 2 * RANK), F32),
            pltpu.VMEM((8 * RANK // 2, 2 * RANK), F32),
            pltpu.VMEM((LEAVES, COLS, points), F32),
            pltpu.VMEM((LEAVES, COLS, points), BF16),
            pltpu.VMEM((LEAVES, COLS, points), BF16),
            pltpu.VMEM((LEAVES // 2, COLS, 2 * RANK), F32),
            pltpu.VMEM((LEAVES // 2, COLS, 2 * RANK), BF16),
            pltpu.VMEM((LEAVES // 2, COLS, 2 * RANK), BF16),
            dma((13,)),
            dma((RING,)),
            dma((RING,)),
            dma((PLANE,)),
            dma((PLANE,)),
            dma((PLANE,)),
            dma((PLANE,)),
            dma((RING,)),
            dma((RING,)),
            dma((5,)),
            dma((5,)),
            dma((5,)),
            dma((5,)),
            dma((2,)),
            dma((2,)),
        ],
        compiler_params=pltpu.CompilerParams(
            collective_id=0, has_side_effects=True, vmem_limit_bytes=60 << 20
        ),
        name="product",
    )(*args)
    return jnp.swapaxes(result, 1, 2)


def solution(mesh):
    placed = (
        P("leaf", None, "sub"),
        P("leaf", "sub", None, None),
        P("leaf", "sub"),
        P("leaf", None, None),
        P("leaf", None, None),
        P("leaf", "sub", None, None),
        P("leaf", "sub"),
        P("leaf", None, None),
        P("leaf", None, None),
        P("leaf", None, None, None),
        P("leaf", None),
        P("leaf", None, None),
        P("leaf", None, None),
        P(),
        P(),
        P(),
        P(),
    )
    return jax.shard_map(
        body, mesh=mesh, in_specs=placed, out_specs=P("leaf", None, "sub"), check_vma=False
    )
```

```python
import jax
import jax.numpy as jnp
from jax import lax
from jax.experimental import pallas as pl
from jax.experimental.pallas import tpu as pltpu
from jax.sharding import PartitionSpec as P

MESH = pl.DeviceIdType.MESH
F32 = jnp.float32
BF16 = jnp.bfloat16

LEAVES = 8
COLS = 16
RANK = 64
RING = 8
PLANE = 16
DEVS = RING * PLANE
TILES = 5
RING_ORDER = (4, 3, 5, 2, 6, 1, 7)
PLANE_ORDER = (10, 6, 14, 9, 11, 2, 8, 5, 7, 13, 15, 1, 3, 4, 12)


def dot(a, b):
    return jnp.dot(a, b, preferred_element_type=F32)


def dot_nt(a, b):
    return lax.dot_general(a, b, (((1,), (1,)), ((), ())), preferred_element_type=F32)


def within(i, first, last):
    return jnp.minimum(jnp.maximum(i, first), last)


def kernel(
    dens_hbm,
    near_hbm,
    near_idx_hbm,
    colb_hbm,
    rowb_hbm,
    lcoup_hbm,
    leaf_idx_hbm,
    lup_hbm,
    ldown_hbm,
    ncoup_hbm,
    node_idx_hbm,
    nup_hbm,
    ndown_hbm,
    upc_hbm,
    upper_idx_hbm,
    upu_hbm,
    upd_hbm,
    out_ref,
    near_idx,
    leaf_idx,
    node_idx,
    upper_idx,
    dens_win,
    near_v,
    colb_v,
    rowb_v,
    lcoup_v,
    lup_v,
    ldown_v,
    ncoup_v,
    nup_v,
    ndown_v,
    upc_v,
    upu_v,
    upd_v,
    lc_win,
    zbuf,
    pbuf,
    rawtab,
    tab,
    last_v,
    sel_up,
    sel_c,
    sel_d,
    near_own,
    near_out,
    near_in,
    far_own,
    far_out,
    far_in,
    load_sem,
    z_send,
    z_recv,
    r_send,
    r_recv,
    p_send,
    p_recv,
    q_send,
    q_recv,
    d_send,
    d_recv,
    l_send,
    l_recv,
    x_send,
    x_recv,
):
    leaf = lax.axis_index("leaf")
    sub = lax.axis_index("sub")
    other = 1 - sub
    group = leaf // RING
    z = leaf % RING
    mid = pl.ds(LEAVES, LEAVES)

    loads = [
        (dens_hbm, dens_win.at[mid, pl.ds(0, COLS), :]),
        (colb_hbm, colb_v),
        (lup_hbm, lup_v),
        (nup_hbm, nup_v),
        (upu_hbm, upu_v),
        (upc_hbm, upc_v),
        (near_hbm, near_v),
        (lcoup_hbm, lcoup_v),
        (upd_hbm, upd_v),
        (ndown_hbm, ndown_v),
        (ncoup_hbm, ncoup_v),
        (ldown_hbm, ldown_v),
        (rowb_hbm, rowb_v),
        (near_idx_hbm, near_idx),
        (leaf_idx_hbm, leaf_idx),
        (node_idx_hbm, node_idx),
        (upper_idx_hbm, upper_idx),
    ]
    load = [
        pltpu.make_async_copy(src, dst, load_sem.at[i]) for i, (src, dst) in enumerate(loads)
    ]
    for copy in load[:5]:
        copy.start()

    def ring_peer(k):
        return {"leaf": group * RING + (z + k) % RING, "sub": sub}

    def plane_peer(k):
        return {"leaf": ((group + k) % PLANE) * RING + z, "sub": sub}

    after, before = (leaf + 1) % DEVS, (leaf + DEVS - 1) % DEVS
    partner = {"leaf": leaf, "sub": other}
    moves = [
        ({"leaf": after, "sub": sub}, LEAVES, 0, 0),
        ({"leaf": before, "sub": sub}, LEAVES, 2 * LEAVES, 0),
        (partner, LEAVES, LEAVES, COLS),
        (partner, 0, 0, COLS),
        (partner, 2 * LEAVES, 2 * LEAVES, COLS),
    ]

    barrier = pltpu.get_barrier_semaphore()
    greeted = (
        [ring_peer(k) for k in RING_ORDER]
        + [plane_peer(k) for k in PLANE_ORDER]
        + [device for device, _, _, _ in moves[:3]]
    )
    for device in greeted:
        pl.semaphore_signal(barrier, inc=1, device_id=device, device_id_type=MESH)

    load[0].wait()
    load[1].wait()
    pairs = []
    for i in range(LEAVES // 2):
        halves = [
            dot_nt(dens_win[LEAVES + t, 0:COLS, :], colb_v[t]) for t in (2 * i, 2 * i + 1)
        ]
        pair = jnp.concatenate(halves, axis=1).astype(BF16)
        lc_win[LEAVES // 2 + i, 0:COLS, :] = pair
        pairs.append(pair)
    load[2].wait()
    load[3].wait()
    for copy in load[5:]:
        copy.start()
    raw = dot(jnp.concatenate(pairs, axis=1), lup_v[...].reshape(LEAVES * RANK, RANK))
    raised = dot(raw.astype(BF16), nup_v[0])
    tile = jnp.concatenate([raw, raised], axis=1).astype(BF16)
    zbuf[z] = tile
    pbuf[group] = tile

    def one_hot(target, count):
        column = lax.broadcasted_iota(jnp.int32, (target.shape[0], count), 1)
        return (column == target).astype(F32).astype(BF16)

    row16 = lax.broadcasted_iota(jnp.int32, (16, 1), 0)
    target = jnp.where(
        row16 < 4,
        60 + 4 * group + row16,
        jnp.where(
            row16 < 6,
            24 + 2 * group + row16,
            jnp.where(row16 == 6, 12 + group, jnp.where(row16 == 7, 4 + group // 2, group // 4)),
        ),
    )
    pick_up = one_hot(target, upu_v.shape[2])
    half = RANK // 2

    def extract(pick, source, dest, rows):
        for r in range(0, half, 2):
            slabs = [source[i] for i in (r, r + half, r + 1, r + 1 + half)]
            both = dot_nt(pick, jnp.concatenate(slabs, axis=0))
            for a in range(2):
                first = (r + a) * rows
                dest[first : first + rows, :] = both[:, 2 * RANK * a : 2 * RANK * (a + 1)]

    load[4].wait()
    extract(pick_up, upu_v, sel_up, 16)

    def matrix_up(k):
        m = sel_up[pl.ds(k, half, stride=16), :]
        return jnp.concatenate([m[:, :RANK], m[:, RANK:]], axis=0)

    blank = jnp.zeros((RANK, RANK), F32)
    up = []
    for k in range(4):
        wide = [matrix_up(k), blank] if k < 2 else [blank, matrix_up(k)]
        up += [jnp.zeros((RANK, 2 * RANK), F32), jnp.concatenate(wide, axis=1)]
    first = jnp.concatenate(up, axis=0).astype(BF16)
    second = [jnp.concatenate([matrix_up(4), matrix_up(5)], axis=0)]
    for k in (6, 7, 8):
        second.append(dot(second[-1].astype(BF16), matrix_up(k).astype(BF16)))
    second = jnp.concatenate(second, axis=1).astype(BF16)
    up = jnp.concatenate([first, dot(first, second).astype(BF16)], axis=1)

    pl.semaphore_wait(barrier, len(greeted))

    def ring_copy(k, slot):
        return pltpu.make_async_remote_copy(
            src_ref=zbuf.at[slot],
            dst_ref=zbuf.at[slot],
            send_sem=z_send.at[k],
            recv_sem=z_recv.at[k],
            device_id=ring_peer(k),
            device_id_type=MESH,
        )

    for k in RING_ORDER:
        ring_copy(k, z).start()

    def raw_copy(k, slot):
        return pltpu.make_async_remote_copy(
            src_ref=pbuf.at[slot],
            dst_ref=pbuf.at[slot],
            send_sem=r_send.at[k],
            recv_sem=r_recv.at[k],
            device_id=plane_peer(k),
            device_id_type=MESH,
        )

    def dens_copy(i):
        device, here, there, row = moves[i]
        return pltpu.make_async_remote_copy(
            src_ref=dens_win.at[pl.ds(here, LEAVES), pl.ds(0, COLS), :],
            dst_ref=dens_win.at[pl.ds(there, LEAVES), pl.ds(row, COLS), :],
            send_sem=d_send.at[i],
            recv_sem=d_recv.at[i],
            device_id=device,
            device_id_type=MESH,
        )

    def lc_copy(i):
        device, here, there, row = moves[i]
        return pltpu.make_async_remote_copy(
            src_ref=lc_win.at[pl.ds(here // 2, LEAVES // 2), pl.ds(0, COLS), :],
            dst_ref=lc_win.at[pl.ds(there // 2, LEAVES // 2), pl.ds(row, COLS), :],
            send_sem=l_send.at[i],
            recv_sem=l_recv.at[i],
            device_id=device,
            device_id_type=MESH,
        )

    for i in range(3):
        lc_copy(i).start()
        dens_copy(i).start()
    for k in PLANE_ORDER:
        raw_copy(k, group).start()

    row8 = lax.broadcasted_iota(jnp.int32, (8, 1), 0)
    top = DEVS + leaf
    node_of = jnp.zeros((8, 1), jnp.int32)
    for k in range(6):
        node_of = jnp.where(row8 == k, top // (2 << k), node_of)
    load[5].wait()
    load[8].wait()
    pick_c = one_hot(node_of - 2, upc_v.shape[3])
    pick_d = one_hot(node_of - 4, upd_v.shape[2])
    for j in range(4):
        extract(pick_c, upc_v.at[j], sel_c.at[j], 8)
    extract(pick_d, upd_v, sel_d, 8)

    load[9].wait()
    chain = [ndown_v[0]]
    for k in range(5):
        m = sel_d[pl.ds(k, half, stride=8), :]
        down = jnp.concatenate([m[:, :RANK], m[:, RANK:]], axis=0).astype(BF16)
        chain.append(dot(chain[-1], down).astype(BF16))

    low = lax.broadcasted_iota(jnp.int32, (COLS, 2 * RANK), 1) < RANK

    def turn(m):
        return jnp.concatenate([m[:, RANK:], m[:, :RANK]], axis=1)

    for k in range(1, RING):
        ring_copy(k, (z + RING - k) % RING).wait_recv()
    c64 = [zbuf[2 * i].astype(F32) + zbuf[2 * i + 1].astype(F32) for i in range(4)]
    sums = dot(jnp.concatenate([c.astype(BF16) for c in c64], axis=1), up)
    tab[group, 0] = jnp.where(low, turn(c64[0]), c64[1]).astype(BF16)
    tab[group, 1] = jnp.where(low, turn(c64[2]), c64[3]).astype(BF16)
    for i in range(3):
        tab[group, 2 + i] = sums[:, 2 * RANK * i : 2 * RANK * (i + 1)].astype(BF16)

    def plane_copy(k, slot):
        return pltpu.make_async_remote_copy(
            src_ref=tab.at[slot],
            dst_ref=tab.at[slot],
            send_sem=p_send.at[k],
            recv_sem=p_recv.at[k],
            device_id=plane_peer(k),
            device_id_type=MESH,
        )

    for k in PLANE_ORDER:
        plane_copy(k, group).start()
    for k in range(1, PLANE):
        raw_copy(k, (group + PLANE - k) % PLANE).wait_recv()
    for i in range(PLANE // 2):
        rawtab[z, i] = jnp.where(
            low, pbuf[2 * i].astype(F32), turn(pbuf[2 * i + 1].astype(F32))
        ).astype(BF16)

    def along_copy(k, slot):
        return pltpu.make_async_remote_copy(
            src_ref=rawtab.at[slot],
            dst_ref=rawtab.at[slot],
            send_sem=q_send.at[k],
            recv_sem=q_recv.at[k],
            device_id=ring_peer(k),
            device_id_type=MESH,
        )

    for k in RING_ORDER:
        along_copy(k, z).start()

    for i in range(2):
        lc_copy(i).wait_recv()
        lc_copy(3 + i).start()
        dens_copy(i).wait_recv()
        dens_copy(3 + i).start()

    low64 = lax.broadcasted_iota(jnp.int32, (half, 2 * RANK), 1) < RANK

    def coupling(k):
        parts = []
        for j in range(4):
            m = sel_c[j, pl.ds(k, half, stride=8), :]
            turned = jnp.concatenate([m[:, RANK:], m[:, :RANK]], axis=1)
            both = [jnp.where(low64, m, turned), jnp.where(low64, turned, m)]
            parts.append(jnp.concatenate(both, axis=0).astype(BF16))
        return jnp.concatenate(parts, axis=1)

    couplings = [coupling(k) for k in range(6)]
    load[10].wait()
    near_coupling = jnp.concatenate([ncoup_v[0, j // 2] for j in range(8)], axis=1)
    load[11].wait()
    load[12].wait()
    points = rowb_v.shape[2]
    for t in range(LEAVES):
        last_v[:, t * points : (t + 1) * points] = lax.dot_general(
            ldown_v[t], rowb_v[t], (((0,), (0,)), ((), ())), preferred_element_type=F32
        ).astype(BF16)

    for i in range(2, 5):
        lc_copy(i).wait_recv()
        dens_copy(i).wait_recv()
    for i in (6, 7, 13, 14, 15, 16):
        load[i].wait()
    base = leaf * LEAVES - LEAVES
    for i in range(LEAVES // 2):
        far = []
        for t in (2 * i, 2 * i + 1):
            near_sum = far_sum = None
            for j in range(3):
                column = within(near_idx[j, t] - base, 0, 3 * LEAVES - 1)
                near_term = dot_nt(dens_win[column], near_v[t, j])
                near_sum = near_term if near_sum is None else near_sum + near_term
                source = within(leaf_idx[j, t] - base, 0, 3 * LEAVES - 1)
                tile = lc_win[source // 2].astype(F32)
                turned = jnp.concatenate([tile[:, RANK:], tile[:, :RANK]], axis=1)
                chosen = jnp.where(source % 2 == 1, turned, tile)[:, :RANK].astype(BF16)
                far_term = dot_nt(chosen, lcoup_v[t, j])
                far_sum = far_term if far_sum is None else far_sum + far_term
            near_own[t] = near_sum[:COLS]
            near_out[t] = near_sum[COLS:].astype(BF16)
            far.append(far_sum)
        pair = jnp.concatenate(far, axis=1)
        far_own[i] = pair[:COLS]
        far_out[i] = pair[COLS:].astype(BF16)

    swaps = [
        pltpu.make_async_remote_copy(
            src_ref=src,
            dst_ref=dst,
            send_sem=x_send.at[i],
            recv_sem=x_recv.at[i],
            device_id=partner,
            device_id_type=MESH,
        )
        for i, (src, dst) in enumerate(((near_out, near_in), (far_out, far_in)))
    ]
    for copy in swaps:
        copy.start()

    for copy in swaps:
        copy.wait_recv()
    for i in range(LEAVES // 2):
        pair = far_own[i] + far_in[i].astype(F32)
        stacked = jnp.concatenate(
            [jnp.where(low, pair, 0.0), jnp.where(low, 0.0, pair)], axis=0
        ).astype(BF16)
        farther = dot(stacked, rowb_v[2 * i : 2 * i + 2].reshape(2 * RANK, points))
        for h in range(2):
            t = 2 * i + h
            near_own[t] += farther[h * COLS : (h + 1) * COLS] + near_in[t].astype(F32)

    for k in range(1, PLANE):
        plane_copy(k, (group + PLANE - k) % PLANE).wait_recv()

    def source_tile(k, j):
        n = within(upper_idx[j, top // (2 << k) - 2], 64 >> k, (128 >> k) - 1)
        if k < 3:
            place = (n - 64) // 4, n % 4 // 2
            if k == 1:
                place = (n - 32) // 2, 2
            if k == 2:
                place = n - 16, 3
            total = tab[place[0], place[1]].astype(F32)
            return jnp.where(low == (n % 2 == 0 if k < 2 else True), total, 0.0).astype(BF16)
        count = 1 << (k - 2)
        first = (n - (64 >> k)) * count
        total = None
        for i in range(count):
            part = tab[first + i, 3 if k == 3 else 4].astype(F32)
            total = part if total is None else total + part
        return jnp.where(low == (k == 4), total, 0.0).astype(BF16)

    def node_tile(j):
        n = within(node_idx[0, j], 0, DEVS - 1)
        tile = rawtab[n % RING, n // (2 * RING)].astype(F32)
        return jnp.where(low == (n // RING % 2 == 0), tile, 0.0).astype(BF16)

    field = None
    for k in range(6):
        part = dot_nt(
            jnp.concatenate([source_tile(k, j) for j in range(4)], axis=1), couplings[k]
        )
        part = dot_nt(part.astype(BF16), chain[k])
        field = part if field is None else field + part
    for k in range(1, RING):
        along_copy(k, (z + RING - k) % RING).wait_recv()
    field = field + dot_nt(
        jnp.concatenate([node_tile(j) for j in range(4)], axis=1), near_coupling
    )
    last = dot(field.astype(BF16), last_v[...])
    for t in range(LEAVES):
        out_ref[t] = (near_own[t] + last[:, t * points : (t + 1) * points]).astype(BF16)

    for k in range(1, RING):
        ring_copy(k, z).wait_send()
        along_copy(k, z).wait_send()
    for k in range(1, PLANE):
        raw_copy(k, group).wait_send()
        plane_copy(k, group).wait_send()
    for i in range(5):
        dens_copy(i).wait_send()
        lc_copy(i).wait_send()
    for copy in swaps:
        copy.wait_send()


def body(
    density,
    near_blocks,
    near_index,
    col_basis,
    row_basis,
    leaf_coupling,
    leaf_list,
    leaf_up,
    leaf_down,
    node_coupling,
    node_list,
    node_up,
    node_down,
    upper_coupling,
    upper_list,
    upper_up,
    upper_down,
):
    args = (
        jnp.swapaxes(density, 1, 2),
        near_blocks,
        near_index.T,
        jnp.swapaxes(col_basis, 1, 2),
        jnp.swapaxes(row_basis, 1, 2),
        leaf_coupling,
        leaf_list.T,
        leaf_up,
        leaf_down,
        node_coupling,
        node_list,
        node_up,
        node_down,
        jnp.transpose(upper_coupling, (1, 2, 3, 0)),
        upper_list.T,
        jnp.transpose(upper_up, (1, 2, 0)),
        jnp.transpose(upper_down, (1, 2, 0)),
    )
    held = pl.BlockSpec(memory_space=pltpu.HBM)
    specs = [held] * len(args)
    points = density.shape[1]
    dma = pltpu.SemaphoreType.DMA

    def like(i):
        return pltpu.VMEM(args[i].shape, args[i].dtype)

    def small(i):
        return pltpu.SMEM(args[i].shape, args[i].dtype)

    result = pl.pallas_call(
        kernel,
        out_shape=pltpu.VMEM((LEAVES, COLS, points), BF16),
        in_specs=specs,
        out_specs=pl.BlockSpec(memory_space=pltpu.VMEM),
        scratch_shapes=[
            small(2),
            small(6),
            small(10),
            small(14),
            pltpu.VMEM((3 * LEAVES, 2 * COLS, points), BF16),
            like(1),
            like(3),
            like(4),
            like(5),
            like(7),
            like(8),
            like(9),
            like(11),
            like(12),
            like(13),
            like(15),
            like(16),
            pltpu.VMEM((3 * LEAVES // 2, 2 * COLS, 2 * RANK), BF16),
            pltpu.VMEM((RING, COLS, 2 * RANK), BF16),
            pltpu.VMEM((PLANE, COLS, 2 * RANK), BF16),
            pltpu.VMEM((RING, PLANE // 2, COLS, 2 * RANK), BF16),
            pltpu.VMEM((PLANE, TILES, COLS, 2 * RANK), BF16),
            pltpu.VMEM((RANK, LEAVES * points), BF16),
            pltpu.VMEM((16 * RANK // 2, 2 * RANK), F32),
            pltpu.VMEM((4, 8 * RANK // 2, 2 * RANK), F32),
            pltpu.VMEM((8 * RANK // 2, 2 * RANK), F32),
            pltpu.VMEM((LEAVES, COLS, points), F32),
            pltpu.VMEM((LEAVES, COLS, points), BF16),
            pltpu.VMEM((LEAVES, COLS, points), BF16),
            pltpu.VMEM((LEAVES // 2, COLS, 2 * RANK), F32),
            pltpu.VMEM((LEAVES // 2, COLS, 2 * RANK), BF16),
            pltpu.VMEM((LEAVES // 2, COLS, 2 * RANK), BF16),
            dma((17,)),
            dma((RING,)),
            dma((RING,)),
            dma((PLANE,)),
            dma((PLANE,)),
            dma((PLANE,)),
            dma((PLANE,)),
            dma((RING,)),
            dma((RING,)),
            dma((5,)),
            dma((5,)),
            dma((5,)),
            dma((5,)),
            dma((2,)),
            dma((2,)),
        ],
        compiler_params=pltpu.CompilerParams(
            collective_id=0, has_side_effects=True, vmem_limit_bytes=60 << 20
        ),
        name="product",
    )(*args)
    return jnp.swapaxes(result, 1, 2)


def solution(mesh):
    placed = (
        P("leaf", None, "sub"),
        P("leaf", "sub", None, None),
        P("leaf", "sub"),
        P("leaf", None, None),
        P("leaf", None, None),
        P("leaf", "sub", None, None),
        P("leaf", "sub"),
        P("leaf", None, None),
        P("leaf", None, None),
        P("leaf", None, None, None),
        P("leaf", None),
        P("leaf", None, None),
        P("leaf", None, None),
        P(),
        P(),
        P(),
        P(),
    )
    return jax.shard_map(
        body, mesh=mesh, in_specs=placed, out_specs=P("leaf", None, "sub"), check_vma=False
    )
```
